32 devices in a mesh: rows: 16 (over z, y, x), cols: 2 (over core).
Axes of the slice: x: 2, y: 2, z: 4, core: 2. Of those that a mesh axis runs over, the one named last changes fastest.
Arguments:
- descriptors: bfloat16 [4096, 1024], P(('rows', 'cols')), may hold values from -6 to 6
- sparse_points: bfloat16 [8192, 1024], P('cols'), may hold values from -6 to 6
- point_scale: float32 [8192], P('cols'), may hold values from 0.3 to 3
- env_owner: int32 [4096, 1], P('rows'), may hold values from 0 to 15; in each aligned block of 128 rows (0 to 127, 128 to 255, ...) at most 12 rows name the same one
- env_structure: int32 [4096], P('rows'), may hold values from 0 to 63
- row_weight: float32 [1024], P('rows'), may hold values from 0.01 to 0.1
- ridge_factor: float32 [1], replicated, may hold values from 0.05 to 0.5
Outputs:
- r_rows: float32 [128, 8192], P(None, 'cols')
- reduced: float32 [1024, 8192], P('rows', 'cols')
The draws below stay inside these ranges and needn't reach their ends.
Inputs may be any that keep to these rules, and one draw needn't show every extreme that they name: `env_owner`: in each aligned block of 128 environments, no owner is named by more than 12 of them.
All inputs are finite; a program needn't handle non-finite values.
Results may differ from the reference program's by a relative error of at most 0.0045.
Values may be sent and summed in bfloat16 or wider, within the bound.
A program may use at most 64 MiB of HBM per device.

```python
import math
import jax
import jax.numpy as jnp
import numpy as np
from jax import lax

DESC = 1024
M = 8192
PW = 64
PANELS = 2
ENV_DEV = 256
EQ_DEV = 64
HALF = 128
CAP = 12
ENV = 4096
NEQ = 1024
N_ROWS = 16


def plant(result, key, least, top_value):
    place = [jax.random.randint(jax.random.fold_in(key, axis), (), 0, length) for axis, length in enumerate(result.shape)]
    widest = result.shape.index(max(result.shape))
    beside = place[:widest] + [(place[widest] + 1) % result.shape[widest]] + place[widest + 1:]
    return result.at[tuple(place)].set(least).at[tuple(beside)].set(top_value)


def level_of(own_key, dims, cuts, low, largest):
    def one(axis_at, parts):
        steps = jax.random.uniform(jax.random.fold_in(jax.random.fold_in(own_key, 6), axis_at), (parts,), jnp.float32, low / len(cuts), largest / len(cuts))
        return jnp.repeat(jnp.exp(steps), dims[axis_at] // parts).reshape((-1,) + (1,) * (len(dims) - axis_at - 1))

    level = one(*cuts[0])
    for cut in cuts[1:]:
        level = level * one(*cut)
    return level


def deal_out(key, own, number, rows, number_of, top, bound, skew):
    ranking = jax.random.permutation(key, number_of)
    crowded, common = shares(number_of, rows * top, bound, skew, True), shares(number_of, rows * top, bound, skew, False)
    places = jnp.arange(number_of)

    def named(lengths, turn):
        used = int((lengths > 0).sum())
        fixed = max(1, used // 4)
        passed = fixed + (places - fixed + turn * (used - fixed)) % max(1, number_of - fixed)
        return jnp.zeros((number_of,), jnp.int32).at[ranking[jnp.where(places < fixed, places, passed)]].set(jnp.asarray(lengths, jnp.int32))

    lengths = jnp.where(number % 4 == 0, named(crowded, number // 4), named(common, number - number // 4 - 1))
    mixed = jax.random.permutation(jax.random.fold_in(own, 3), number_of)
    source_of, sink = mixed[0:number_of // 2 * 2:2], mixed[1:number_of // 2 * 2:2]
    room = jnp.minimum(lengths[source_of] - 1, bound - lengths[sink]) // 2
    room = jnp.where((source_of == ranking[0]) | (sink == ranking[0]) | (lengths[sink] == 0), 0, jnp.maximum(room, 0))
    passed = jax.random.randint(jax.random.fold_in(own, 4), (number_of // 2,), 0, 1 << 20) % (room + 1)
    lengths = lengths.at[source_of].add(-passed).at[sink].add(passed)
    items = jnp.searchsorted(jnp.cumsum(lengths), jnp.arange(rows * top), side="right").astype(jnp.int32)
    grid = items.reshape(top, rows).T
    grid = grid[jax.random.permutation(jax.random.fold_in(own, 1), rows)]
    turn = jax.random.randint(jax.random.fold_in(own, 2), (rows, 1), 0, top)
    return jnp.take_along_axis(grid, (jnp.arange(top)[None, :] + turn) % top, axis=1)


def shares(amount, total, bound, skew, full):
    weights = [(1 << 20) // math.isqrt(rank ** skew) + 1 for rank in range(1, amount + 1)]
    largest = bound if full else min(bound, max(-(-total // amount), total * weights[0] // sum(weights)))
    least = 1 if total - largest >= amount - 1 else 0
    counts, rest = [largest] + [least] * (amount - 1), total - largest - least * (amount - 1)
    while rest > 0:
        free = [i for i in range(1, amount) if counts[i] < largest] or [i for i in range(1, amount) if counts[i] < bound]
        pool, left = sum([weights[i] for i in free]), rest
        for i in free:
            extra = min(bound - counts[i], max(1, left * weights[i] // pool), rest)
            counts[i] = counts[i] + extra
            rest = rest - extra
    return np.array(counts)


def scatter_about(stream_key, shape, scale, reach, shards=(), kind=jnp.bfloat16):
    array = jax.random.normal(stream_key, shape, jnp.float32) * scale
    if len(shards) > 0:
        array = level_of(stream_key, shape, shards, -0.22, 0.18) * array
    return jnp.clip(array, min=-reach, max=reach).astype(kind)


def setup_inputs(seed: int = 0) -> dict:
    key_list = jax.random.split(jax.random.key(seed), 8)
    descriptors = scatter_about(key_list[0], (ENV, DESC), 1.0, 6.0, ((0, 32),))
    sparse_points = scatter_about(key_list[1], (M, DESC), 1.0, 6.0, ((0, 2),))
    point_scale = jnp.clip(jnp.exp(math.log(3.0) - 2.3025851 * jax.random.uniform(key_list[2], (M,), jnp.float32) ** level_of(key_list[2], (M,), ((0, 2),), -0.2, 0.2)), 0.3, 3.0)
    env_owner_keys = jax.random.split(jax.random.fold_in(key_list[3], 1), ENV // HALF)
    env_owner_turns = jax.random.permutation(jax.random.fold_in(key_list[3], 3), ENV // HALF)
    env_owner = jax.vmap(lambda own, number: deal_out(jax.random.fold_in(key_list[3], 2), own, number, HALF, N_ROWS, 1, CAP, 2))(env_owner_keys, env_owner_turns).reshape((ENV, 1))
    env_structure = plant(jax.random.randint(key_list[4], (ENV,), 0, EQ_DEV), jax.random.fold_in(key_list[4], 1), 0, EQ_DEV - 1).astype(jnp.int32)
    row_weight = jnp.clip(jnp.exp(math.log(0.1) - 2.3025851 * jax.random.uniform(key_list[5], (NEQ,), jnp.float32) ** level_of(key_list[5], (NEQ,), ((0, 16),), -0.2, 0.2)), 0.01, 0.1)
    ridge_factor = jnp.clip(jnp.exp(jax.random.uniform(key_list[6], (1,), jnp.float32, math.log(0.05), math.log(0.5))), 0.05, 0.5)
    return {"descriptors": descriptors, "sparse_points": sparse_points, "point_scale": point_scale, "env_owner": env_owner, "env_structure": env_structure, "row_weight": row_weight, "ridge_factor": ridge_factor}


def inner_cols(left, right):
    return lax.dot_general(left.astype(jnp.float32), right.astype(jnp.float32), (((0,), (0,)), ((), ())), precision=lax.Precision.HIGHEST, preferred_element_type=jnp.float32)

def factor(gram_mat, ridge_factor):
    shift = ridge_factor[0] * jnp.trace(gram_mat) / PW + 1e-06
    chol_lower = jnp.linalg.cholesky(gram_mat + shift * jnp.eye(PW, dtype=jnp.float32))
    inverse = jax.scipy.linalg.solve_triangular(chol_lower, jnp.eye(PW, dtype=jnp.float32), lower=True)
    return (chol_lower, inverse)

def reference(descriptors, sparse_points, point_scale, env_owner, env_structure, row_weight, ridge_factor):
    dot_scale = DESC ** (-0.5)
    points = sparse_points.astype(jnp.float32)
    global_ids = (env_owner[:, 0].astype(jnp.int32) * EQ_DEV + env_structure.astype(jnp.int32)).astype(jnp.int32)
    desc_blocks = descriptors.reshape(N_ROWS, ENV_DEV, DESC)
    id_blocks = global_ids.reshape(N_ROWS, ENV_DEV)

    def add_block(sums, pieces):
        env_rows, env_ids = pieces
        products = jnp.dot(env_rows.astype(jnp.float32), points.T.astype(jnp.float32), precision=lax.Precision.HIGHEST, preferred_element_type=jnp.float32) * dot_scale
        squared = products * products
        kernel = (point_scale[None, :] * squared * squared).astype(jnp.bfloat16)
        kernel = lax.optimization_barrier(kernel).astype(jnp.float32)
        return (sums + jax.ops.segment_sum(kernel, env_ids, num_segments=NEQ), None)
    sums, _ = lax.scan(add_block, jnp.zeros((NEQ, M), jnp.float32), (desc_blocks, id_blocks))
    matrix = sums * row_weight[:, None]
    col_ids = jnp.arange(M, dtype=jnp.int32)[None, :]
    norm_scale = 1.0 / NEQ ** 0.5
    r_blocks = []
    for panel_idx in range(PANELS):
        first_col = panel_idx * PW
        panel_cols = matrix[:, first_col:first_col + PW]
        chol_lower, inverse = factor(inner_cols(panel_cols, panel_cols), ridge_factor)
        q_cols = jnp.dot(panel_cols.astype(jnp.float32), inverse.T.astype(jnp.float32), precision=lax.Precision.HIGHEST, preferred_element_type=jnp.float32)
        coupled = inner_cols(q_cols, matrix)
        later_mask = col_ids >= first_col + PW
        inside = (col_ids >= first_col) & (col_ids < first_col + PW)
        coupled = jnp.where(later_mask, coupled, 0.0)
        update = jnp.dot(q_cols.astype(jnp.float32), coupled.astype(jnp.float32), precision=lax.Precision.HIGHEST, preferred_element_type=jnp.float32)
        q_wide = jnp.pad(q_cols, ((0, 0), (first_col, M - first_col - PW)))
        matrix = jnp.where(inside, q_wide, matrix - update)
        r_wide = jnp.pad(chol_lower.T, ((0, 0), (first_col, M - first_col - PW)))
        r_blocks.append(jnp.where(inside, r_wide, coupled) * norm_scale)
    return (jnp.concatenate(r_blocks, axis=0), matrix)
```

```python
import functools
import math

import jax
import jax.numpy as jnp
from jax import lax
from jax.experimental import pallas as pl
from jax.experimental.pallas import tpu as pltpu
from jax.sharding import PartitionSpec as P

PW = 64
PANELS = 2
WIDE = PW * PANELS
BLOCK = 128
LANES = 128
PIVOTS = 8
HI = lax.Precision.HIGHEST
F32 = jnp.float32
BF16 = jnp.bfloat16
MESH = pl.DeviceIdType.MESH


def mm(left, right, contract, precision=HI):
    return lax.dot_general(
        left, right, ((contract[0], contract[1]), ((), ())), precision=precision,
        preferred_element_type=F32,
    )


def eliminate(system):
    rows = lax.broadcasted_iota(jnp.int32, (PW, WIDE), 0)
    for k in range(0, PW, PIVOTS):
        rest, index = system[k:], rows[k:]
        cols = [
            jnp.broadcast_to(rest[:, k + j:k + j + 1], rest.shape) for j in range(PIVOTS)
        ]
        tops = [rest[j:j + 1] for j in range(PIVOTS)]
        for p in range(PIVOTS):
            mult = jnp.where(index > k + p, cols[p] * (1.0 / cols[p][p:p + 1]), 0.0)
            for j in range(p + 1, PIVOTS):
                cols[j] = cols[j] - mult * cols[j][p:p + 1]
                tops[j] = tops[j] - mult[j:j + 1] * tops[p]
            cols[p] = mult
        for p in range(PIVOTS):
            rest = rest - cols[p] * tops[p]
        system = jnp.concatenate([system[:k], rest], axis=0) if k else rest
    return system


def factor(gram, ridge):
    row = lax.broadcasted_iota(jnp.int32, (PW, PW), 0)
    col = lax.broadcasted_iota(jnp.int32, (PW, PW), 1)
    on = row == col
    trace = jnp.sum(jnp.sum(jnp.where(on, gram, 0.0), axis=1, keepdims=True), axis=0, keepdims=True)
    shift = ridge * trace / PW + 1e-06
    eye = on.astype(F32)
    system = eliminate(jnp.concatenate([gram + shift * eye, eye], axis=1))
    left = system[:, :PW]
    diag = jnp.sum(jnp.where(on, left, 0.0), axis=1, keepdims=True)
    scale = lax.rsqrt(diag)
    upper = jnp.where(col >= row, left * scale, 0.0)
    return upper, system[:, PW:] * scale, shift


def bit_of(index, bit):
    return (index // (1 << bit)) % 2


def split_bf16(value):
    high = value.astype(BF16)
    return high, (value - high.astype(F32)).astype(BF16)


def fit_kernel(
    owners, units, env_ref, label_ref, points_hbm, scale_ref, head_points_ref, head_scale_ref,
    weight_ref, ridge_ref,
    coupled_hbm, matrix_hbm, q_ref, r_head_ref,
    points, matrix, gram_out, gram_in, gram_sum, gram_all, acc, sent, got, whole,
    points_sem, out_sem, g_send, g_recv, h_send, h_recv, r_send, r_recv,
):
    me = lax.axis_index("rows")
    stages = owners.bit_length() - 1
    eq_count = weight_ref.shape[0]
    env_count, desc = env_ref.shape
    col_count = scale_ref.shape[1]
    unit_cols = col_count // units
    grow = WIDE // owners
    high = unit_cols // owners
    row_parts = WIDE // high

    loads = []
    for u in range(units):
        load = pltpu.make_async_copy(
            points_hbm.at[pl.ds(u * unit_cols, unit_cols)], points.at[u], points_sem.at[u]
        )
        load.start()
        loads.append(load)

    barrier = pltpu.get_barrier_semaphore()

    def greet(d, _):
        pl.semaphore_signal(
            barrier, inc=1, device_id={"rows": (me + d) % owners}, device_id_type=MESH
        )
        return 0

    lax.fori_loop(1, owners, greet, 0)

    env_rows = env_ref[...]
    targets = lax.broadcasted_iota(jnp.int32, (eq_count, env_count), 0)
    selector = jnp.where(label_ref[...] == targets, 1.0, 0.0).astype(BF16)
    weight = weight_ref[...]

    def equations(rows, scale):
        products = mm(env_rows, rows, ((1,), (1,)), None) * desc ** (-0.5)
        squared = products * products
        kernel = (scale * squared * squared).astype(BF16)
        return mm(selector, kernel, ((1,), (0,)), None) * weight

    head = equations(head_points_ref[...], head_scale_ref[...])
    gram = mm(head, head, ((0,), (0,)))
    for p in range(owners):
        gram_out[p] = gram[p * grow:(p + 1) * grow]
    pl.semaphore_wait(barrier, owners - 1)

    def spread(src_of, slots, send, recv):
        def start(d, _):
            to = (me + d) % owners
            pltpu.make_async_remote_copy(
                src_ref=src_of(to), dst_ref=slots.at[me], send_sem=send.at[to],
                recv_sem=recv.at[me], device_id={"rows": to}, device_id_type=MESH,
            ).start()
            return 0

        lax.fori_loop(1, owners, start, 0)

    def collect(src_of, slots, send, recv):
        def end(d, _):
            other = (me + d) % owners
            copy = pltpu.make_async_remote_copy(
                src_ref=src_of(other), dst_ref=slots.at[other], send_sem=send.at[other],
                recv_sem=recv.at[other], device_id={"rows": other}, device_id_type=MESH,
            )
            copy.wait_send()
            copy.wait_recv()
            return 0

        lax.fori_loop(1, owners, end, 0)

    spread(lambda to: gram_out.at[to], gram_in, g_send, g_recv)
    gram_in[me] = gram_out[me]

    def unit_matrix(u):
        loads[u].wait()
        cols = slice(u * unit_cols, (u + 1) * unit_cols)
        matrix[u] = equations(points[u], scale_ref[:, cols])
        out = pltpu.make_async_copy(matrix.at[u], matrix_hbm.at[u], out_sem.at[0, u])
        out.start()
        return out

    outs = []
    for u in range(units // 2):
        outs.append(unit_matrix(u))
    collect(lambda to: gram_out.at[to], gram_in, g_send, g_recv)
    total = gram_in[0]
    for p in range(1, owners):
        total = total + gram_in[p]
    gram_sum[...] = total
    spread(lambda to: gram_sum, gram_all, h_send, h_recv)
    gram_all[me] = total
    for u in range(units // 2, units):
        outs.append(unit_matrix(u))
    collect(lambda to: gram_sum, gram_all, h_send, h_recv)
    gram = jnp.concatenate([gram_all[p] for p in range(owners)], axis=0)

    ridge = ridge_ref[...]
    up1, inv1, shift = factor(gram[:PW, :PW], ridge)
    c12 = mm(inv1, gram[:PW, PW:], ((1,), (0,)))
    back = mm(inv1, c12, ((0,), (0,)))
    pair = jnp.concatenate([c12, jnp.sqrt(shift) * back], axis=0)
    up2, inv2, _ = factor(gram[PW:, PW:] - mm(pair, pair, ((0,), (0,))), ridge)
    q1 = mm(head[:, :PW], inv1, ((1,), (1,)))
    q2 = mm(head[:, PW:] - mm(q1, c12, ((1,), (0,))), inv2, ((1,), (1,)))
    deep = c12 + shift * mm(inv1, back, ((1,), (0,)))
    w2 = mm(head[:, PW:] - mm(q1, deep, ((1,), (0,))), inv2, ((1,), (1,)))
    q_ref[...] = jnp.concatenate([q1, q2], axis=1)
    r_head_ref[...] = jnp.concatenate(
        [
            jnp.concatenate([up1, c12], axis=1),
            jnp.concatenate([jnp.zeros((PW, PW), F32), up2], axis=1),
        ],
        axis=0,
    )
    w_high, w_low = split_bf16(jnp.concatenate([q1, w2], axis=1).T)
    w_wide = jnp.concatenate([w_high, w_low, w_high], axis=1)

    def order(u):
        bits = list(range(stages))
        if u % 2 and stages > 1:
            bits[0], bits[1] = 1, 0
        return bits

    def start_of(u, t):
        bits = order(u)
        return sum(
            (bit_of(me, bits[i]) * (owners >> (i + 1)) for i in range(t)), jnp.int32(0)
        )

    def reduce_copy(u, t):
        mine = bit_of(me, order(u)[t])
        half = owners >> (t + 1)
        step = 1 << order(u)[t]
        first = start_of(u, t) + (1 - mine) * half
        return pltpu.make_async_remote_copy(
            src_ref=sent.at[u, pl.ds(first, half)],
            dst_ref=got.at[u, pl.ds(owners - 2 * half, half)],
            send_sem=r_send.at[u, t], recv_sem=r_recv.at[u, t],
            device_id={"rows": me + (1 - 2 * mine) * step}, device_id_type=MESH,
        )

    def gather_copy(u, t):
        mine = bit_of(me, order(u)[t])
        half = owners >> (t + 1)
        step = 1 << order(u)[t]
        first = start_of(u, t + 1)
        return pltpu.make_async_remote_copy(
            src_ref=whole.at[u, pl.ds(first, half)],
            dst_ref=whole.at[u, pl.ds(first, half)],
            send_sem=r_send.at[u, stages + t], recv_sem=r_recv.at[u, stages + t],
            device_id={"rows": me + (1 - 2 * mine) * step}, device_id_type=MESH,
        )

    def open_unit(u):
        m_high, m_low = split_bf16(matrix[u])
        part = mm(
            w_wide, jnp.concatenate([m_high, m_high, m_low], axis=0), ((1,), (0,)), None
        )
        for p in range(owners):
            row, col = (p % row_parts) * high, (p // row_parts) * LANES
            piece = part[row:row + high, col:col + LANES]
            acc[u, p] = piece
            sent[u, p] = piece.astype(BF16)
        reduce_copy(u, 0).start()

    def reduce_step(u, t):
        copy = reduce_copy(u, t)
        copy.wait_recv()
        half = owners >> (t + 1)
        keep = start_of(u, t + 1)
        value = acc[u, pl.ds(keep, half)] + got[
            u, pl.ds(owners - 2 * half, half)
        ].astype(F32)
        if t + 1 < stages:
            acc[u, pl.ds(keep, half)] = value
            sent[u, pl.ds(keep, half)] = value.astype(BF16)
            reduce_copy(u, t + 1).start()
        else:
            whole[u, pl.ds(keep, half)] = value.astype(BF16)
            gather_copy(u, t).start()

    def gather_step(u, t):
        gather_copy(u, t).wait_recv()
        if t:
            gather_copy(u, t - 1).start()
        else:
            out = pltpu.make_async_copy(whole.at[u], coupled_hbm.at[u], out_sem.at[1, u])
            out.start()
            outs.append(out)

    def run(u, s):
        if s == 0:
            open_unit(u)
        elif s <= stages:
            reduce_step(u, s - 1)
        else:
            gather_step(u, 2 * stages - s)

    lag = 2
    steps = 2 * stages + 1
    for wave in range(steps + lag * ((units - 1) // 2)):
        for u in range(units):
            s = wave - lag * (u // 2)
            if 0 <= s < steps:
                run(u, s)
    for u in range(units):
        for t in range(stages):
            reduce_copy(u, t).wait_send()
            gather_copy(u, t).wait_send()
    for out in outs:
        out.wait()


def fit(env_rows, labels, points, scale, head_points, head_scale, row_weight, ridge, owners, units):
    col_count, desc = points.shape
    unit_cols = col_count // units
    eq_count = row_weight.shape[0]
    high = unit_cols // owners
    stages = owners.bit_length() - 1
    grow = WIDE // owners
    vmem = pl.BlockSpec(memory_space=pltpu.VMEM)
    hbm = pl.BlockSpec(memory_space=pl.ANY)
    dma = pltpu.SemaphoreType.DMA
    return pl.pallas_call(
        functools.partial(fit_kernel, owners, units),
        out_shape=(
            jax.ShapeDtypeStruct((units, owners, high, LANES), BF16),
            jax.ShapeDtypeStruct((units, eq_count, unit_cols), F32),
            jax.ShapeDtypeStruct((eq_count, WIDE), F32),
            jax.ShapeDtypeStruct((WIDE, WIDE), F32),
        ),
        in_specs=[vmem, vmem, hbm, vmem, vmem, vmem, vmem, vmem],
        out_specs=(hbm, hbm, vmem, vmem),
        scratch_shapes=[
            pltpu.VMEM((units, unit_cols, desc), BF16),
            pltpu.VMEM((units, eq_count, unit_cols), F32),
            pltpu.VMEM((owners, grow, WIDE), F32),
            pltpu.VMEM((owners, grow, WIDE), F32),
            pltpu.VMEM((grow, WIDE), F32),
            pltpu.VMEM((owners, grow, WIDE), F32),
            pltpu.VMEM((units, owners, high, LANES), F32),
            pltpu.VMEM((units, owners, high, LANES), BF16),
            pltpu.VMEM((units, owners, high, LANES), BF16),
            pltpu.VMEM((units, owners, high, LANES), BF16),
            dma((units,)),
            dma((2, units)),
            dma((owners,)),
            dma((owners,)),
            dma((owners,)),
            dma((owners,)),
            dma((units, 2 * stages)),
            dma((units, 2 * stages)),
        ],
        compiler_params=pltpu.CompilerParams(collective_id=0, has_side_effects=True),
    )(
        env_rows, labels.reshape(1, -1), points, scale.reshape(1, -1), head_points,
        head_scale.reshape(1, -1), row_weight.reshape(-1, 1), ridge.reshape(1, 1),
    )


def finish_kernel(norm_scale, coupled_ref, matrix_ref, q_ref, r_head_ref, r_ref, reduced_ref):
    owners, high, _ = coupled_ref.shape[1:]
    row_parts = WIDE // high
    cols = [
        jnp.concatenate([coupled_ref[0, c * row_parts + r] for r in range(row_parts)], axis=0)
        for c in range(owners // row_parts)
    ]
    coupled = jnp.concatenate(cols, axis=1)
    q_cols = q_ref[...]
    q_high, q_low = split_bf16(q_cols)
    update = mm(
        jnp.concatenate([q_high, q_low], axis=1), jnp.concatenate([coupled, coupled], axis=0),
        ((1,), (0,)), None,
    )
    r_ref[...] = coupled.astype(F32) * norm_scale
    reduced_ref[...] = matrix_ref[0] - update

    @pl.when((lax.axis_index("cols") == 0) & (pl.program_id(0) == 0))
    def _():
        r_ref[:, :WIDE] = r_head_ref[...] * norm_scale
        reduced_ref[:, :WIDE] = q_cols


def finish(coupled, matrix, q_cols, r_head, norm_scale):
    units, owners, high, _ = coupled.shape
    _, eq_count, unit_cols = matrix.shape
    return pl.pallas_call(
        functools.partial(finish_kernel, norm_scale),
        grid=(units,),
        out_shape=(
            jax.ShapeDtypeStruct((WIDE, units * unit_cols), F32),
            jax.ShapeDtypeStruct((eq_count, units * unit_cols), F32),
        ),
        in_specs=[
            pl.BlockSpec((1, owners, high, LANES), lambda u: (u, 0, 0, 0)),
            pl.BlockSpec((1, eq_count, unit_cols), lambda u: (u, 0, 0)),
            pl.BlockSpec((eq_count, WIDE), lambda u: (0, 0)),
            pl.BlockSpec((WIDE, WIDE), lambda u: (0, 0)),
        ],
        out_specs=(
            pl.BlockSpec((WIDE, unit_cols), lambda u: (0, u)),
            pl.BlockSpec((eq_count, unit_cols), lambda u: (0, u)),
        ),
    )(coupled, matrix, q_cols, r_head)


def from_root(value, axis):
    return lax.all_gather(value, axis)[0]


def body(
    descriptors, sparse_points, point_scale, env_owner, env_structure, row_weight, ridge_factor
):
    owners = lax.axis_size("rows")
    col_index = lax.axis_index("cols")
    eq_count = row_weight.shape[0]
    env_local, desc = descriptors.shape
    col_count = sparse_points.shape[0]

    head_points = from_root(sparse_points[:WIDE], "cols")
    head_scale = from_root(point_scale[:WIDE], "cols")

    per_block = max(2, (3 * BLOCK + 2 * owners - 1) // (2 * owners))
    capacity = min(env_local, per_block * (-(-env_local // BLOCK)))
    own = lax.dynamic_slice_in_dim(env_owner[:, 0], col_index * env_local, env_local)
    struct = lax.dynamic_slice_in_dim(env_structure, col_index * env_local, env_local)
    idx = jnp.arange(env_local)
    within = jnp.sum(
        ((own[:, None] == own[None, :]) & (idx[None, :] < idx[:, None])).astype(jnp.int32), axis=1
    )
    slot = own * capacity + within
    slots = lax.broadcasted_iota(jnp.int32, (owners * capacity, env_local), 0)
    pick = (slots == slot[None, :]).astype(BF16)
    lane = lax.broadcasted_iota(jnp.int32, (env_local, LANES), 1)
    tag = jnp.where(lane == 0, struct[:, None] + 1, 0).astype(BF16)
    payload = mm(
        pick, jnp.concatenate([descriptors, tag], axis=1), ((1,), (0,)), None
    ).astype(BF16)
    arrived = lax.all_to_all(payload, "rows", 0, 0, tiled=True)
    arrived = lax.all_gather(arrived, "cols", axis=0, tiled=True)
    env_rows = arrived[:, :desc]
    labels = arrived[:, desc].astype(jnp.int32) - 1

    units = max(1, min(8, col_count // (16 * owners)))
    coupled, matrix, q_cols, r_head = fit(
        env_rows, labels, sparse_points, point_scale, head_points, head_scale, row_weight,
        ridge_factor, owners, units,
    )
    return finish(coupled, matrix, q_cols, r_head, 1.0 / math.sqrt(owners * eq_count))


def solution(mesh):
    return jax.shard_map(
        body,
        mesh=mesh,
        in_specs=(
            P(("rows", "cols"), None),
            P("cols", None),
            P("cols"),
            P("rows", None),
            P("rows"),
            P("rows"),
            P(),
        ),
        out_specs=(P(None, "cols"), P("rows", "cols")),
        check_vma=False,
    )
```

```python
import functools
import math

import jax
import jax.numpy as jnp
from jax import lax
from jax.experimental import pallas as pl
from jax.experimental.pallas import tpu as pltpu
from jax.sharding import PartitionSpec as P

PW = 64
PANELS = 2
WIDE = PW * PANELS
BLOCK = 128
LANES = 128
PIVOTS = 8
UNITS = 4
LAG = 0.3
HI = lax.Precision.HIGHEST
F32 = jnp.float32
BF16 = jnp.bfloat16
MESH = pl.DeviceIdType.MESH


def mm(left, right, contract, precision=HI):
    return lax.dot_general(
        left, right, ((contract[0], contract[1]), ((), ())), precision=precision,
        preferred_element_type=F32,
    )


def eliminate(system):
    rows = lax.broadcasted_iota(jnp.int32, (PW, WIDE), 0)
    for k in range(0, PW, PIVOTS):
        rest, index = system[k:], rows[k:]
        cols = [
            jnp.broadcast_to(rest[:, k + j:k + j + 1], rest.shape) for j in range(PIVOTS)
        ]
        tops = [rest[j:j + 1] for j in range(PIVOTS)]
        for p in range(PIVOTS):
            mult = jnp.where(index > k + p, cols[p] * (1.0 / cols[p][p:p + 1]), 0.0)
            for j in range(p + 1, PIVOTS):
                cols[j] = cols[j] - mult * cols[j][p:p + 1]
                tops[j] = tops[j] - mult[j:j + 1] * tops[p]
            cols[p] = mult
        for p in range(PIVOTS):
            rest = rest - cols[p] * tops[p]
        system = jnp.concatenate([system[:k], rest], axis=0) if k else rest
    return system


def factor(gram, ridge):
    row = lax.broadcasted_iota(jnp.int32, (PW, PW), 0)
    col = lax.broadcasted_iota(jnp.int32, (PW, PW), 1)
    on = row == col
    trace = jnp.sum(jnp.sum(jnp.where(on, gram, 0.0), axis=1, keepdims=True), axis=0, keepdims=True)
    shift = ridge * trace / PW + 1e-06
    eye = on.astype(F32)
    system = eliminate(jnp.concatenate([gram + shift * eye, eye], axis=1))
    left = system[:, :PW]
    diag = jnp.sum(jnp.where(on, left, 0.0), axis=1, keepdims=True)
    scale = lax.rsqrt(diag)
    upper = jnp.where(col >= row, left * scale, 0.0)
    return upper, system[:, PW:] * scale, shift


def bit_of(index, bit):
    return (index // (1 << bit)) % 2


def split_bf16(value):
    high = value.astype(BF16)
    return high, (value - high.astype(F32)).astype(BF16)


def fit_kernel(
    owners, cores, units, groups, tail,
    desc_ref, owner_ref, struct_ref, points_hbm, scale_ref, weight_ref, ridge_ref,
    coupled_hbm, matrix_hbm, q_ref, r_head_ref,
    points, head_points, head_scale, keys, parcel, landed, env, matrix,
    gram_out, gram_in, gram_sum, gram_all, acc, sent, got, spot, whole,
    points_sem, out_sem, root_sem, root_send, root_recv, e_send, e_recv, f_send, f_recv,
    g_send, g_recv, h_send, h_recv, r_send, r_recv,
):
    me = lax.axis_index("rows")
    core = lax.axis_index("cols")
    env_local, desc = desc_ref.shape
    eq_count = weight_ref.shape[1]
    col_count = scale_ref.shape[1]
    unit_cols = col_count // units
    grow = WIDE // owners
    high = unit_cols // owners
    row_parts = WIDE // high
    line = owners // 4
    half_desc = desc // 2

    barrier = pltpu.get_barrier_semaphore()

    def greet_rows(d, _):
        pl.semaphore_signal(
            barrier, inc=1, device_id={"rows": (me + d) % owners}, device_id_type=MESH
        )
        return 0

    def greet_cols(d, _):
        pl.semaphore_signal(
            barrier, inc=1, device_id={"cols": (core + d) % cores}, device_id_type=MESH
        )
        return 0

    lax.fori_loop(1, owners, greet_rows, 0)
    lax.fori_loop(1, cores, greet_cols, 0)

    loads = []
    for u in range(units):
        load = pltpu.make_async_copy(
            points_hbm.at[pl.ds(u * unit_cols, unit_cols)], points.at[u], points_sem.at[u]
        )
        load.start()
        loads.append(load)

    def as_column(row):
        return jnp.broadcast_to(row.astype(F32), (LANES, row.shape[1])).T

    keys[0] = as_column(owner_ref[...])
    keys[1] = as_column(struct_ref[...])
    mine = pl.ds(pl.multiple_of(core * env_local, 8), env_local)
    own, struct = keys[0, mine], keys[1, mine]
    lane = lax.broadcasted_iota(jnp.int32, (env_local, LANES), 1).astype(F32)
    named = own == lane
    before = (
        lax.broadcasted_iota(jnp.int32, (env_local, env_local), 0)
        > lax.broadcasted_iota(jnp.int32, (env_local, env_local), 1)
    )
    ahead = mm(
        jnp.where(before, 1.0, 0.0).astype(BF16), jnp.where(named, 1.0, 0.0).astype(BF16),
        ((1,), (0,)), None,
    )
    within = jnp.sum(jnp.where(named, ahead, 0.0), axis=1, keepdims=True)
    own, struct = own[:, :1], struct[:, :1]
    place = lax.broadcasted_iota(jnp.int32, (env_local, owners * 8), 1).astype(F32)

    def pick(first, count, shift):
        inside = (within >= first) & (within < first + count)
        spot_of = jnp.where(inside, own * 8 + (within - first) + shift, -1.0)
        return jnp.where(place == spot_of, 1.0, 0.0).astype(BF16)

    descriptors = desc_ref[...]
    label = jnp.zeros((owners * 8, LANES), F32)
    for g in range(groups):
        chosen = pick(8 * g, 8, 0)
        block = mm(chosen, descriptors, ((0,), (0,)), None)
        parcel[:, :, g * desc:(g + 1) * desc] = block.reshape(owners, 8, desc).astype(BF16)
        tag = jnp.where(lane == g, struct + 1.0, 0.0).astype(BF16)
        label = label + mm(chosen, tag, ((0,), (0,)), None)
    edge = groups * desc
    if tail:
        lower, upper = pick(8 * groups, 4, 0), pick(8 * groups, 4, 4)
        block = mm(lower, descriptors[:, :half_desc], ((0,), (0,)), None) + mm(
            upper, descriptors[:, half_desc:], ((0,), (0,)), None
        )
        parcel[:, :, edge:edge + half_desc] = block.reshape(owners, 8, half_desc).astype(BF16)
        tag = jnp.where(lane == groups, struct + 1.0, 0.0).astype(BF16)
        label = label + mm(lower, tag, ((0,), (0,)), None)
        edge = edge + half_desc
    parcel[:, :, edge:] = label.reshape(owners, 8, LANES).astype(BF16)

    pl.semaphore_wait(barrier, owners + cores - 2)

    def exchange(src_of, slot_of, send, recv):
        def copy(to, sender):
            return pltpu.make_async_remote_copy(
                src_ref=src_of(to), dst_ref=slot_of(sender), send_sem=send.at[to],
                recv_sem=recv.at[sender], device_id={"rows": to}, device_id_type=MESH,
            )

        def start(d, _):
            copy((me + d) % owners, me).start()
            return 0

        def end(d, _):
            other = (me + d) % owners
            copy(other, other).wait_send()
            copy(other, other).wait_recv()
            return 0

        return start, end, copy

    start, _, routed = exchange(
        lambda to: parcel.at[to], lambda sender: landed.at[core, sender], e_send, e_recv
    )
    lax.fori_loop(1, owners, start, 0)

    def root_copies(to):
        pair = []
        for i, (src, dst) in enumerate(
            ((points_hbm.at[pl.ds(0, WIDE)], head_points), (scale_ref.at[:, pl.ds(0, WIDE)], head_scale))
        ):
            pair.append(
                pltpu.make_async_remote_copy(
                    src_ref=src, dst_ref=dst, send_sem=root_send.at[i, to],
                    recv_sem=root_recv.at[i], device_id={"cols": to}, device_id_type=MESH,
                )
            )
        return pair

    own_points = pltpu.make_async_copy(points_hbm.at[pl.ds(0, WIDE)], head_points, root_sem)

    @pl.when(core == 0)
    def _():
        own_points.start()
        head_scale[...] = scale_ref[:, :WIDE]
        for to in range(1, cores):
            for copy in root_copies(to):
                copy.start()

    def pass_on(slot, to, sender):
        return pltpu.make_async_remote_copy(
            src_ref=landed.at[sender, slot], dst_ref=landed.at[sender, slot],
            send_sem=f_send.at[to, slot], recv_sem=f_recv.at[sender, slot],
            device_id={"cols": to}, device_id_type=MESH,
        )

    def pass_all(slot):
        def one(d, _):
            pass_on(slot, (core + d) % cores, core).start()
            return 0

        lax.fori_loop(1, cores, one, 0)

    landed[core, me] = parcel[me]
    pass_all(me)

    def land(d, _):
        other = (me + d) % owners
        routed(other, other).wait_recv()
        pass_all(other)
        return 0

    lax.fori_loop(1, owners, land, 0)

    @pl.when(core == 0)
    def _():
        own_points.wait()
        for to in range(1, cores):
            for copy in root_copies(to):
                copy.wait_send()

    @pl.when(core != 0)
    def _():
        for copy in root_copies(0):
            copy.wait_recv()

    def passed(i, _):
        slot = i % owners
        other = (core + 1 + i // owners) % cores
        pass_on(slot, other, other).wait_recv()
        return 0

    lax.fori_loop(0, owners * (cores - 1), passed, 0)

    targets = lax.broadcasted_iota(jnp.int32, (1, LANES), 1).astype(F32)
    low_half = lax.broadcasted_iota(jnp.int32, (owners // 2, 8, 1), 1) < 4
    marks = []
    row = 0

    def swap(value):
        return jnp.concatenate([value[:, 4:], value[:, :4]], axis=1)

    def evens(value):
        paired = value.reshape((owners // 2, 2) + value.shape[1:])
        return paired[:, 0], paired[:, 1]

    for c in range(cores):
        tags = landed[c, :, :, edge:].astype(F32)
        for g in range(groups):
            env[row:row + owners * 8] = landed[c, :, :, g * desc:(g + 1) * desc].astype(
                F32
            ).reshape(owners * 8, desc).astype(BF16)
            tag = tags[:, :, g:g + 1].reshape(owners * 8, 1) - 1.0
            marks.append(jnp.where(tag == targets, 1.0, 0.0))
            row += owners * 8
        if tail:
            first, second = evens(
                landed[c, :, :, groups * desc:groups * desc + half_desc].astype(F32)
            )
            left = jnp.where(low_half, first, swap(second))
            right = jnp.where(low_half, swap(first), second)
            env[row:row + owners * 4, :half_desc] = left.reshape(owners * 4, half_desc).astype(BF16)
            env[row:row + owners * 4, half_desc:] = right.reshape(owners * 4, half_desc).astype(BF16)
            first, second = evens(jnp.broadcast_to(tags[:, :, groups:groups + 1], tags.shape))
            tag = jnp.where(low_half, first, swap(second)).reshape(owners * 4, LANES) - 1.0
            marks.append(jnp.where(tag == targets, 1.0, 0.0))
            row += owners * 4
    selector = jnp.concatenate(marks, axis=0).T[:eq_count].astype(BF16)
    weight = as_column(weight_ref[...])[:, :1]

    def equations(rows, scale):
        products = mm(env[...], rows, ((1,), (1,)), None) * desc ** (-0.5)
        squared = products * products
        kernel = (scale * squared * squared).astype(BF16)
        return mm(selector, kernel, ((1,), (0,)), None) * weight

    head = equations(head_points[...], head_scale[...])
    gram = mm(head, head, ((0,), (0,)))
    for p in range(owners):
        gram_out[p] = gram[p * grow:(p + 1) * grow]
    start, end, _ = exchange(
        lambda to: gram_out.at[to], lambda sender: gram_in.at[sender], g_send, g_recv
    )
    lax.fori_loop(1, owners, start, 0)
    gram_in[me] = gram_out[me]

    outs = []

    def unit_matrix(u):
        loads[u].wait()
        cols = slice(u * unit_cols, (u + 1) * unit_cols)
        matrix[u] = equations(points[u], scale_ref[:, cols])
        out = pltpu.make_async_copy(matrix.at[u], matrix_hbm.at[u], out_sem.at[0, u])
        out.start()
        outs.append(out)

    for u in range(units // 2):
        unit_matrix(u)
    lax.fori_loop(1, owners, end, 0)
    total = gram_in[0]
    for p in range(1, owners):
        total = total + gram_in[p]
    gram_sum[...] = total
    start, end, _ = exchange(
        lambda to: gram_sum, lambda sender: gram_all.at[sender], h_send, h_recv
    )
    lax.fori_loop(1, owners, start, 0)
    gram_all[me] = total
    for u in range(units // 2, units):
        unit_matrix(u)
    lax.fori_loop(1, owners, end, 0)
    gram = jnp.concatenate([gram_all[p] for p in range(owners)], axis=0)

    ridge = ridge_ref[...]
    up1, inv1, shift = factor(gram[:PW, :PW], ridge)
    c12 = mm(inv1, gram[:PW, PW:], ((1,), (0,)))
    back = mm(inv1, c12, ((0,), (0,)))
    pair = jnp.concatenate([c12, jnp.sqrt(shift) * back], axis=0)
    up2, inv2, _ = factor(gram[PW:, PW:] - mm(pair, pair, ((0,), (0,))), ridge)
    q1 = mm(head[:, :PW], inv1, ((1,), (1,)))
    q2 = mm(head[:, PW:] - mm(q1, c12, ((1,), (0,))), inv2, ((1,), (1,)))
    deep = c12 + shift * mm(inv1, back, ((1,), (0,)))
    w2 = mm(head[:, PW:] - mm(q1, deep, ((1,), (0,))), inv2, ((1,), (1,)))
    q_ref[...] = jnp.concatenate([q1, q2], axis=1)
    r_head_ref[...] = jnp.concatenate(
        [
            jnp.concatenate([up1, c12], axis=1),
            jnp.concatenate([jnp.zeros((PW, PW), F32), up2], axis=1),
        ],
        axis=0,
    )
    w_high, w_low = split_bf16(jnp.concatenate([q1, w2], axis=1).T)
    w_wide = jnp.concatenate([w_high, w_low, w_high], axis=1)

    rank = me // 4

    def bit(u, t):
        return (t + u) % 2

    def start_of(u, t):
        return sum(
            (bit_of(me, bit(u, i)) * (owners >> (i + 1)) for i in range(t)), jnp.int32(0)
        )

    def peer(u, t):
        return me + (1 - 2 * bit_of(me, bit(u, t))) * (1 << bit(u, t))

    def reduce_copy(u, t):
        half = owners >> (t + 1)
        first = start_of(u, t) + (1 - bit_of(me, bit(u, t))) * half
        return pltpu.make_async_remote_copy(
            src_ref=sent.at[u, pl.ds(first, half)],
            dst_ref=got.at[u, pl.ds(owners - 2 * half, half)],
            send_sem=r_send.at[u, t], recv_sem=r_recv.at[u, t],
            device_id={"rows": peer(u, t)}, device_id_type=MESH,
        )

    def gather_copy(u, t):
        half = owners >> (t + 1)
        part = whole.at[u, pl.ds(start_of(u, t + 1), half)]
        return pltpu.make_async_remote_copy(
            src_ref=part, dst_ref=part, send_sem=r_send.at[u, 2 + t],
            recv_sem=r_recv.at[u, 2 + t], device_id={"rows": peer(u, t)}, device_id_type=MESH,
        )

    def line_reduce(u, to, sender):
        return pltpu.make_async_remote_copy(
            src_ref=sent.at[u, start_of(u, 2) + to], dst_ref=spot.at[u, sender],
            send_sem=r_send.at[u, 4 + to], recv_sem=r_recv.at[u, 4 + sender],
            device_id={"rows": to * 4 + me % 4}, device_id_type=MESH,
        )

    def line_gather(u, to, sender):
        part = whole.at[u, start_of(u, 2) + sender]
        return pltpu.make_async_remote_copy(
            src_ref=part, dst_ref=part, send_sem=r_send.at[u, 4 + line + to],
            recv_sem=r_recv.at[u, 4 + line + sender],
            device_id={"rows": to * 4 + me % 4}, device_id_type=MESH,
        )

    def others():
        return [(rank + d) % line for d in range(1, line)]

    def open_unit(u):
        m_high, m_low = split_bf16(matrix[u])
        part = mm(
            w_wide, jnp.concatenate([m_high, m_high, m_low], axis=0), ((1,), (0,)), None
        )
        for p in range(owners):
            r, c = (p % row_parts) * high, (p // row_parts) * LANES
            piece = part[r:r + high, c:c + LANES]
            acc[u, p] = piece
            sent[u, p] = piece.astype(BF16)
        reduce_copy(u, 0).start()

    def reduce_step(u, t):
        reduce_copy(u, t).wait_recv()
        half = owners >> (t + 1)
        keep = pl.ds(start_of(u, t + 1), half)
        value = acc[u, keep] + got[u, pl.ds(owners - 2 * half, half)].astype(F32)
        acc[u, keep] = value
        sent[u, keep] = value.astype(BF16)
        if t == 0:
            reduce_copy(u, 1).start()
        else:
            for to in others():
                line_reduce(u, to, rank).start()

    def line_step(u):
        mine_at = start_of(u, 2) + rank
        value = acc[u, mine_at]
        for other in others():
            line_reduce(u, other, other).wait_recv()
            value = value + spot[u, other].astype(F32)
        whole[u, mine_at] = value.astype(BF16)
        for to in others():
            line_gather(u, to, rank).start()

    def line_end(u):
        for other in others():
            line_gather(u, other, other).wait_recv()
        gather_copy(u, 1).start()

    def gather_step(u, t):
        gather_copy(u, t).wait_recv()
        if t:
            gather_copy(u, 0).start()
        else:
            out = pltpu.make_async_copy(whole.at[u], coupled_hbm.at[u], out_sem.at[1, u])
            out.start()
            outs.append(out)

    steps = (
        open_unit, lambda u: reduce_step(u, 0), lambda u: reduce_step(u, 1), line_step, line_end,
        lambda u: gather_step(u, 1), lambda u: gather_step(u, 0),
    )
    plan = sorted(
        (s + LAG * (u // 2), u, s) for u in range(units) for s in range(len(steps))
    )
    for _, u, s in plan:
        steps[s](u)

    for u in range(units):
        for t in range(2):
            reduce_copy(u, t).wait_send()
            gather_copy(u, t).wait_send()
        for to in others():
            line_reduce(u, to, rank).wait_send()
            line_gather(u, to, rank).wait_send()
    for out in outs:
        out.wait()

    def drain(d, _):
        other = (me + d) % owners
        routed(other, other).wait_send()
        return 0

    lax.fori_loop(1, owners, drain, 0)

    def drain_pass(i, _):
        pass_on(i % owners, (core + 1 + i // owners) % cores, core).wait_send()
        return 0

    lax.fori_loop(0, owners * (cores - 1), drain_pass, 0)


def fit(descriptors, owner, struct, points, scale, row_weight, ridge, owners, cores, units, capacity):
    col_count, desc = points.shape
    unit_cols = col_count // units
    eq_count = row_weight.shape[0]
    high = unit_cols // owners
    grow = WIDE // owners
    left = capacity % 8
    tail = 0 < left <= 4
    groups = capacity // 8 + (left > 4)
    span = groups * desc + (desc // 2 if tail else 0) + LANES
    env_count = cores * owners * (8 * groups + 4 * tail)
    line = owners // 4
    vmem = pl.BlockSpec(memory_space=pltpu.VMEM)
    hbm = pl.BlockSpec(memory_space=pl.ANY)
    dma = pltpu.SemaphoreType.DMA
    return pl.pallas_call(
        functools.partial(fit_kernel, owners, cores, units, groups, tail),
        out_shape=(
            jax.ShapeDtypeStruct((units, owners, high, LANES), BF16),
            jax.ShapeDtypeStruct((units, eq_count, unit_cols), F32),
            jax.ShapeDtypeStruct((eq_count, WIDE), F32),
            jax.ShapeDtypeStruct((WIDE, WIDE), F32),
        ),
        in_specs=[vmem, vmem, vmem, hbm, vmem, vmem, vmem],
        out_specs=(hbm, hbm, vmem, vmem),
        scratch_shapes=[
            pltpu.VMEM((units, unit_cols, desc), BF16),
            pltpu.VMEM((WIDE, desc), BF16),
            pltpu.VMEM((1, WIDE), F32),
            pltpu.VMEM((2, owner.shape[0], LANES), F32),
            pltpu.VMEM((owners, 8, span), BF16),
            pltpu.VMEM((cores, owners, 8, span), BF16),
            pltpu.VMEM((env_count, desc), BF16),
            pltpu.VMEM((units, eq_count, unit_cols), F32),
            pltpu.VMEM((owners, grow, WIDE), F32),
            pltpu.VMEM((owners, grow, WIDE), F32),
            pltpu.VMEM((grow, WIDE), F32),
            pltpu.VMEM((owners, grow, WIDE), F32),
            pltpu.VMEM((units, owners, high, LANES), F32),
            pltpu.VMEM((units, owners, high, LANES), BF16),
            pltpu.VMEM((units, owners, high, LANES), BF16),
            pltpu.VMEM((units, line, high, LANES), BF16),
            pltpu.VMEM((units, owners, high, LANES), BF16),
            dma((units,)),
            dma((2, units)),
            dma,
            dma((2, cores)),
            dma((2,)),
            dma((owners,)),
            dma((owners,)),
            dma((cores, owners)),
            dma((cores, owners)),
            dma((owners,)),
            dma((owners,)),
            dma((owners,)),
            dma((owners,)),
            dma((units, 4 + 2 * line)),
            dma((units, 4 + 2 * line)),
        ],
        compiler_params=pltpu.CompilerParams(collective_id=0, has_side_effects=True),
    )(
        descriptors, owner.reshape(1, -1), struct.reshape(1, -1), points, scale.reshape(1, -1),
        row_weight.reshape(1, -1), ridge.reshape(1, 1),
    )


def finish_kernel(norm_scale, coupled_ref, matrix_ref, q_ref, r_head_ref, r_ref, reduced_ref):
    units, owners, high, _ = coupled_ref.shape
    unit_cols = matrix_ref.shape[2]
    row_parts = WIDE // high
    q_cols = q_ref[...]
    q_high, q_low = split_bf16(q_cols)
    q_wide = jnp.concatenate([q_high, q_low], axis=1)
    for u in range(units):
        cols = [
            jnp.concatenate(
                [coupled_ref[u, c * row_parts + r] for r in range(row_parts)], axis=0
            )
            for c in range(owners // row_parts)
        ]
        coupled = jnp.concatenate(cols, axis=1)
        update = mm(q_wide, jnp.concatenate([coupled, coupled], axis=0), ((1,), (0,)), None)
        at = slice(u * unit_cols, (u + 1) * unit_cols)
        r_ref[:, at] = coupled.astype(F32) * norm_scale
        reduced_ref[:, at] = matrix_ref[u] - update

    @pl.when((lax.axis_index("cols") == 0) & (pl.program_id(0) == 0))
    def _():
        r_ref[:, :WIDE] = r_head_ref[...] * norm_scale
        reduced_ref[:, :WIDE] = q_cols


def finish(coupled, matrix, q_cols, r_head, norm_scale):
    units, owners, high, _ = coupled.shape
    _, eq_count, unit_cols = matrix.shape
    each = max(1, units // 2)
    return pl.pallas_call(
        functools.partial(finish_kernel, norm_scale),
        grid=(units // each,),
        out_shape=(
            jax.ShapeDtypeStruct((WIDE, units * unit_cols), F32),
            jax.ShapeDtypeStruct((eq_count, units * unit_cols), F32),
        ),
        in_specs=[
            pl.BlockSpec((each, owners, high, LANES), lambda u: (u, 0, 0, 0)),
            pl.BlockSpec((each, eq_count, unit_cols), lambda u: (u, 0, 0)),
            pl.BlockSpec((eq_count, WIDE), lambda u: (0, 0)),
            pl.BlockSpec((WIDE, WIDE), lambda u: (0, 0)),
        ],
        out_specs=(
            pl.BlockSpec((WIDE, each * unit_cols), lambda u: (0, u)),
            pl.BlockSpec((eq_count, each * unit_cols), lambda u: (0, u)),
        ),
    )(coupled, matrix, q_cols, r_head)


def body(
    descriptors, sparse_points, point_scale, env_owner, env_structure, row_weight, ridge_factor
):
    owners, cores = lax.axis_size("rows"), lax.axis_size("cols")
    eq_count = row_weight.shape[0]
    env_local = descriptors.shape[0]
    col_count = sparse_points.shape[0]
    per_block = max(2, (3 * BLOCK + 2 * owners - 1) // (2 * owners))
    capacity = min(env_local, per_block * (-(-env_local // BLOCK)))
    units = max(1, min(UNITS, col_count // (16 * owners)))
    coupled, matrix, q_cols, r_head = fit(
        descriptors, env_owner, env_structure, sparse_points, point_scale, row_weight,
        ridge_factor, owners, cores, units, capacity,
    )
    return finish(coupled, matrix, q_cols, r_head, 1.0 / math.sqrt(owners * eq_count))


def solution(mesh):
    return jax.shard_map(
        body,
        mesh=mesh,
        in_specs=(
            P(("rows", "cols"), None),
            P("cols", None),
            P("cols"),
            P("rows", None),
            P("rows"),
            P("rows"),
            P(),
        ),
        out_specs=(P(None, "cols"), P("rows", "cols")),
        check_vma=False,
    )
```

```python
import functools
import math

import jax
import jax.numpy as jnp
from jax import lax
from jax.experimental import pallas as pl
from jax.experimental.pallas import tpu as pltpu
from jax.sharding import PartitionSpec as P

PW = 64
PANELS = 2
WIDE = PW * PANELS
BLOCK = 128
LANES = 128
PIVOTS = 8
UNITS = 2
HI = lax.Precision.HIGHEST
F32 = jnp.float32
BF16 = jnp.bfloat16
MESH = pl.DeviceIdType.MESH


def mm(left, right, contract, precision=HI):
    return lax.dot_general(
        left, right, ((contract[0], contract[1]), ((), ())), precision=precision,
        preferred_element_type=F32,
    )


def eliminate(system):
    rows = lax.broadcasted_iota(jnp.int32, (PW, WIDE), 0)
    for k in range(0, PW, PIVOTS):
        rest, index = system[k:], rows[k:]
        cols = [
            jnp.broadcast_to(rest[:, k + j:k + j + 1], rest.shape) for j in range(PIVOTS)
        ]
        tops = [rest[j:j + 1] for j in range(PIVOTS)]
        for p in range(PIVOTS):
            mult = jnp.where(index > k + p, cols[p] * (1.0 / cols[p][p:p + 1]), 0.0)
            for j in range(p + 1, PIVOTS):
                cols[j] = cols[j] - mult * cols[j][p:p + 1]
                tops[j] = tops[j] - mult[j:j + 1] * tops[p]
            cols[p] = mult
        for p in range(PIVOTS):
            rest = rest - cols[p] * tops[p]
        system = jnp.concatenate([system[:k], rest], axis=0) if k else rest
    return system


def factor(gram, ridge):
    row = lax.broadcasted_iota(jnp.int32, (PW, PW), 0)
    col = lax.broadcasted_iota(jnp.int32, (PW, PW), 1)
    on = row == col
    trace = jnp.sum(jnp.sum(jnp.where(on, gram, 0.0), axis=1, keepdims=True), axis=0, keepdims=True)
    shift = ridge * trace / PW + 1e-06
    eye = on.astype(F32)
    system = eliminate(jnp.concatenate([gram + shift * eye, eye], axis=1))
    left = system[:, :PW]
    diag = jnp.sum(jnp.where(on, left, 0.0), axis=1, keepdims=True)
    scale = lax.rsqrt(diag)
    upper = jnp.where(col >= row, left * scale, 0.0)
    return upper, system[:, PW:] * scale, shift


def bit_of(index, bit):
    return (index // (1 << bit)) % 2


def split_bf16(value):
    high = value.astype(BF16)
    return high, (value - high.astype(F32)).astype(BF16)


def fit_kernel(
    owners, cores, units, groups, tail,
    desc_ref, owner_ref, struct_ref, points_hbm, scale_ref, weight_ref, ridge_ref,
    coupled_hbm, matrix_hbm, q_ref, r_head_ref,
    points, head_points, head_scale, keys, parcel, landed, env, matrix,
    head_out, heads, block_out, block_in, whole,
    points_sem, out_sem, root_sem, root_send, root_recv, e_send, e_recv, f_send, f_recv,
    h_send, h_recv, k_send, k_recv, b_send, b_recv, r_send, r_recv,
):
    me = lax.axis_index("rows")
    core = lax.axis_index("cols")
    env_local, desc = desc_ref.shape
    eq_count = weight_ref.shape[1]
    col_count = scale_ref.shape[1]
    unit_cols = col_count // units
    width = unit_cols // owners
    lanes = block_in.shape[3]
    share = eq_count // cores
    line = owners // 4
    half_desc = desc // 2

    barrier = pltpu.get_barrier_semaphore()

    def greet_rows(d, _):
        pl.semaphore_signal(
            barrier, inc=1, device_id={"rows": (me + d) % owners}, device_id_type=MESH
        )
        return 0

    def greet_cols(d, _):
        pl.semaphore_signal(
            barrier, inc=1, device_id={"cols": (core + d) % cores}, device_id_type=MESH
        )
        return 0

    lax.fori_loop(1, owners, greet_rows, 0)
    lax.fori_loop(1, cores, greet_cols, 0)

    loads = []
    for u in range(units):
        load = pltpu.make_async_copy(
            points_hbm.at[pl.ds(u * unit_cols, unit_cols)], points.at[u], points_sem.at[u]
        )
        load.start()
        loads.append(load)

    def as_column(row):
        return jnp.broadcast_to(row.astype(F32), (LANES, row.shape[1])).T

    keys[0] = as_column(owner_ref[...])
    keys[1] = as_column(struct_ref[...])
    mine = pl.ds(pl.multiple_of(core * env_local, 8), env_local)
    own, struct = keys[0, mine], keys[1, mine]
    lane = lax.broadcasted_iota(jnp.int32, (env_local, LANES), 1).astype(F32)
    named = own == lane
    before = (
        lax.broadcasted_iota(jnp.int32, (env_local, env_local), 0)
        > lax.broadcasted_iota(jnp.int32, (env_local, env_local), 1)
    )
    ahead = mm(
        jnp.where(before, 1.0, 0.0).astype(BF16), jnp.where(named, 1.0, 0.0).astype(BF16),
        ((1,), (0,)), None,
    )
    within = jnp.sum(jnp.where(named, ahead, 0.0), axis=1, keepdims=True)
    own, struct = own[:, :1], struct[:, :1]
    place = lax.broadcasted_iota(jnp.int32, (env_local, owners * 8), 1).astype(F32)

    def pick(first, count, shift):
        inside = (within >= first) & (within < first + count)
        spot_of = jnp.where(inside, own * 8 + (within - first) + shift, -1.0)
        return jnp.where(place == spot_of, 1.0, 0.0).astype(BF16)

    descriptors = desc_ref[...]
    label = jnp.zeros((owners * 8, LANES), F32)
    for g in range(groups):
        chosen = pick(8 * g, 8, 0)
        block = mm(chosen, descriptors, ((0,), (0,)), None)
        parcel[:, :, g * desc:(g + 1) * desc] = block.reshape(owners, 8, desc).astype(BF16)
        tag = jnp.where(lane == g, struct + 1.0, 0.0).astype(BF16)
        label = label + mm(chosen, tag, ((0,), (0,)), None)
    edge = groups * desc
    if tail:
        lower, upper = pick(8 * groups, 4, 0), pick(8 * groups, 4, 4)
        block = mm(lower, descriptors[:, :half_desc], ((0,), (0,)), None) + mm(
            upper, descriptors[:, half_desc:], ((0,), (0,)), None
        )
        parcel[:, :, edge:edge + half_desc] = block.reshape(owners, 8, half_desc).astype(BF16)
        tag = jnp.where(lane == groups, struct + 1.0, 0.0).astype(BF16)
        label = label + mm(lower, tag, ((0,), (0,)), None)
        edge = edge + half_desc
    parcel[:, :, edge:] = label.reshape(owners, 8, LANES).astype(BF16)

    pl.semaphore_wait(barrier, owners + cores - 2)

    def exchange(src_of, slot_of, send, recv):
        def copy(to, sender):
            return pltpu.make_async_remote_copy(
                src_ref=src_of(to), dst_ref=slot_of(sender), send_sem=send.at[to],
                recv_sem=recv.at[sender], device_id={"rows": to}, device_id_type=MESH,
            )

        def start(d, _):
            copy((me + d) % owners, me).start()
            return 0

        def end(d, _):
            other = (me + d) % owners
            copy(other, other).wait_send()
            copy(other, other).wait_recv()
            return 0

        return start, end, copy

    start, _, routed = exchange(
        lambda to: parcel.at[to], lambda sender: landed.at[core, sender], e_send, e_recv
    )
    lax.fori_loop(1, owners, start, 0)

    def root_copies(to):
        pair = []
        for i, (src, dst) in enumerate(
            ((points_hbm.at[pl.ds(0, WIDE)], head_points), (scale_ref.at[:, pl.ds(0, WIDE)], head_scale))
        ):
            pair.append(
                pltpu.make_async_remote_copy(
                    src_ref=src, dst_ref=dst, send_sem=root_send.at[i, to],
                    recv_sem=root_recv.at[i], device_id={"cols": to}, device_id_type=MESH,
                )
            )
        return pair

    own_points = pltpu.make_async_copy(points_hbm.at[pl.ds(0, WIDE)], head_points, root_sem)

    @pl.when(core == 0)
    def _():
        own_points.start()
        head_scale[...] = scale_ref[:, :WIDE]
        for to in range(1, cores):
            for copy in root_copies(to):
                copy.start()

    def pass_on(slot, to, sender):
        return pltpu.make_async_remote_copy(
            src_ref=landed.at[sender, slot], dst_ref=landed.at[sender, slot],
            send_sem=f_send.at[to, slot], recv_sem=f_recv.at[sender, slot],
            device_id={"cols": to}, device_id_type=MESH,
        )

    def pass_all(slot):
        def one(d, _):
            pass_on(slot, (core + d) % cores, core).start()
            return 0

        lax.fori_loop(1, cores, one, 0)

    landed[core, me] = parcel[me]
    pass_all(me)

    def land(d, _):
        other = (me + d) % owners
        routed(other, other).wait_recv()
        pass_all(other)
        return 0

    lax.fori_loop(1, owners, land, 0)

    @pl.when(core == 0)
    def _():
        own_points.wait()
        for to in range(1, cores):
            for copy in root_copies(to):
                copy.wait_send()

    @pl.when(core != 0)
    def _():
        for copy in root_copies(0):
            copy.wait_recv()

    def passed(i, _):
        slot = i % owners
        other = (core + 1 + i // owners) % cores
        pass_on(slot, other, other).wait_recv()
        return 0

    lax.fori_loop(0, owners * (cores - 1), passed, 0)

    targets = lax.broadcasted_iota(jnp.int32, (1, LANES), 1).astype(F32)
    low_half = lax.broadcasted_iota(jnp.int32, (owners // 2, 8, 1), 1) < 4
    marks = []
    row = 0

    def swap(value):
        return jnp.concatenate([value[:, 4:], value[:, :4]], axis=1)

    def evens(value):
        paired = value.reshape((owners // 2, 2) + value.shape[1:])
        return paired[:, 0], paired[:, 1]

    for c in range(cores):
        tags = landed[c, :, :, edge:].astype(F32)
        for g in range(groups):
            env[row:row + owners * 8] = landed[c, :, :, g * desc:(g + 1) * desc].astype(
                F32
            ).reshape(owners * 8, desc).astype(BF16)
            tag = tags[:, :, g:g + 1].reshape(owners * 8, 1) - 1.0
            marks.append(jnp.where(tag == targets, 1.0, 0.0))
            row += owners * 8
        if tail:
            first, second = evens(
                landed[c, :, :, groups * desc:groups * desc + half_desc].astype(F32)
            )
            left = jnp.where(low_half, first, swap(second))
            right = jnp.where(low_half, swap(first), second)
            env[row:row + owners * 4, :half_desc] = left.reshape(owners * 4, half_desc).astype(BF16)
            env[row:row + owners * 4, half_desc:] = right.reshape(owners * 4, half_desc).astype(BF16)
            first, second = evens(jnp.broadcast_to(tags[:, :, groups:groups + 1], tags.shape))
            tag = jnp.where(low_half, first, swap(second)).reshape(owners * 4, LANES) - 1.0
            marks.append(jnp.where(tag == targets, 1.0, 0.0))
            row += owners * 4
    selector = jnp.concatenate(marks, axis=0).T[:eq_count].astype(BF16)
    weight = as_column(weight_ref[...])[:, :1]

    def equations(rows, scale):
        products = mm(env[...], rows, ((1,), (1,)), None) * desc ** (-0.5)
        squared = products * products
        kernel = (scale * squared * squared).astype(BF16)
        return mm(selector, kernel, ((1,), (0,)), None) * weight

    head = equations(head_points[...], head_scale[...])
    for c in range(cores):
        head_out[c] = head[c * share:(c + 1) * share]
    start, _, shared = exchange(
        lambda to: head_out.at[core], lambda sender: heads.at[sender, core], h_send, h_recv
    )
    lax.fori_loop(1, owners, start, 0)
    heads[me] = head_out[...]

    outs = []
    blocks = []
    for u in range(units):
        loads[u].wait()
        value = equations(points[u], scale_ref[:, u * unit_cols:(u + 1) * unit_cols])
        matrix[u] = value
        out = pltpu.make_async_copy(matrix.at[u], matrix_hbm.at[u], out_sem.at[0, u])
        out.start()
        outs.append(out)
        value = value.astype(BF16)
        for p in range(owners):
            block_out[u, p, :, :width] = value[:, p * width:(p + 1) * width]
        start, end, _ = exchange(
            lambda to, u=u: block_out.at[u, to], lambda sender, u=u: block_in.at[u, sender],
            b_send.at[u], b_recv.at[u],
        )
        lax.fori_loop(1, owners, start, 0)
        block_in[u, me] = block_out[u, me]
        blocks.append(end)

    def hand_head(slot, to, sender):
        part = heads.at[slot, sender]
        return pltpu.make_async_remote_copy(
            src_ref=part, dst_ref=part, send_sem=k_send.at[to, slot],
            recv_sem=k_recv.at[sender, slot], device_id={"cols": to}, device_id_type=MESH,
        )

    def land_head(d, _):
        other = (me + d) % owners
        shared(other, other).wait_recv()

        def one(e, _):
            hand_head(other, (core + e) % cores, core).start()
            return 0

        lax.fori_loop(1, cores, one, 0)
        return 0

    lax.fori_loop(1, owners, land_head, 0)

    def handed(i, _):
        other = (core + 1 + i // (owners - 1)) % cores
        hand_head((me + 1 + i % (owners - 1)) % owners, other, other).wait_recv()
        return 0

    lax.fori_loop(0, (owners - 1) * (cores - 1), handed, 0)

    every = heads[...].reshape(owners * eq_count, WIDE)
    gram = mm(every, every, ((0,), (0,)))
    ridge = ridge_ref[...]
    up1, inv1, shift = factor(gram[:PW, :PW], ridge)

    rank = me // 4

    def bit(u, t):
        return (t + u) % 2

    def start_of(u, t):
        return sum(
            (bit_of(me, bit(u, i)) * (owners >> (i + 1)) for i in range(t)), jnp.int32(0)
        )

    def gather_copy(u, k, t):
        half = owners >> (t + 1)
        part = whole.at[u, k, pl.ds(start_of(u, t + 1), half)]
        to = me + (1 - 2 * bit_of(me, bit(u, t))) * (1 << bit(u, t))
        return pltpu.make_async_remote_copy(
            src_ref=part, dst_ref=part, send_sem=r_send.at[u, k, t],
            recv_sem=r_recv.at[u, k, t], device_id={"rows": to}, device_id_type=MESH,
        )

    def line_copy(u, k, to, sender):
        part = whole.at[u, k, start_of(u, 2) + sender]
        return pltpu.make_async_remote_copy(
            src_ref=part, dst_ref=part, send_sem=r_send.at[u, k, 2 + to],
            recv_sem=r_recv.at[u, k, 2 + sender],
            device_id={"rows": to * 4 + me % 4}, device_id_type=MESH,
        )

    others = [(rank + d) % line for d in range(1, line)]

    def open_piece(u, k, value):
        whole[u, k, start_of(u, 2) + rank] = value.astype(BF16)
        for to in others:
            line_copy(u, k, to, rank).start()

    def line_end(u, k):
        for other in others:
            line_copy(u, k, other, other).wait_recv()
        gather_copy(u, k, 1).start()

    def middle(u, k):
        gather_copy(u, k, 1).wait_recv()
        gather_copy(u, k, 0).start()

    def last(u, k):
        gather_copy(u, k, 0).wait_recv()
        out = pltpu.make_async_copy(whole.at[u, k], coupled_hbm.at[u, k], out_sem.at[1 + k, u])
        out.start()
        outs.append(out)

    crosses, firsts = [], []
    for u in range(units):
        lax.fori_loop(1, owners, blocks[u], 0)
        cross = mm(
            every, block_in[u].reshape(owners * eq_count, lanes).astype(F32), ((0,), (0,))
        )
        first = mm(inv1, cross[:PW], ((1,), (0,)))
        open_piece(u, 0, first)
        crosses.append(cross)
        firsts.append(first)

    c12 = mm(inv1, gram[:PW, PW:], ((1,), (0,)))
    back = mm(inv1, c12, ((0,), (0,)))
    pair = jnp.concatenate([c12, jnp.sqrt(shift) * back], axis=0)
    deep = c12 + shift * mm(inv1, back, ((1,), (0,)))
    up2, inv2, _ = factor(gram[PW:, PW:] - mm(pair, pair, ((0,), (0,))), ridge)
    for u in range(units):
        rest = crosses[u][PW:] - mm(deep, firsts[u], ((0,), (0,)))
        open_piece(u, 1, mm(inv2, rest, ((1,), (0,))))

    q1 = mm(head[:, :PW], inv1, ((1,), (1,)))
    q2 = mm(head[:, PW:] - mm(q1, c12, ((1,), (0,))), inv2, ((1,), (1,)))
    q_ref[...] = jnp.concatenate([q1, q2], axis=1)
    r_head_ref[...] = jnp.concatenate(
        [
            jnp.concatenate([up1, c12], axis=1),
            jnp.concatenate([jnp.zeros((PW, PW), F32), up2], axis=1),
        ],
        axis=0,
    )

    for k in range(PANELS):
        for u in range(units):
            line_end(u, k)
    for k in range(PANELS):
        for u in range(units):
            middle(u, k)
    for k in range(PANELS):
        for u in range(units):
            last(u, k)

    for u in range(units):
        for k in range(PANELS):
            for t in range(2):
                gather_copy(u, k, t).wait_send()
            for to in others:
                line_copy(u, k, to, rank).wait_send()
    for out in outs:
        out.wait()

    def drain(d, _):
        other = (me + d) % owners
        routed(other, other).wait_send()
        shared(other, other).wait_send()
        return 0

    lax.fori_loop(1, owners, drain, 0)

    def drain_pass(i, _):
        pass_on(i % owners, (core + 1 + i // owners) % cores, core).wait_send()
        return 0

    lax.fori_loop(0, owners * (cores - 1), drain_pass, 0)

    def drain_head(i, _):
        to = (core + 1 + i // (owners - 1)) % cores
        hand_head((me + 1 + i % (owners - 1)) % owners, to, core).wait_send()
        return 0

    lax.fori_loop(0, (owners - 1) * (cores - 1), drain_head, 0)


def fit(descriptors, owner, struct, points, scale, row_weight, ridge, owners, cores, units, capacity):
    col_count, desc = points.shape
    unit_cols = col_count // units
    eq_count = row_weight.shape[0]
    lanes = max(LANES, unit_cols // owners)
    left = capacity % 8
    tail = 0 < left <= 4
    groups = capacity // 8 + (left > 4)
    span = groups * desc + (desc // 2 if tail else 0) + LANES
    env_count = cores * owners * (8 * groups + 4 * tail)
    line = owners // 4
    vmem = pl.BlockSpec(memory_space=pltpu.VMEM)
    hbm = pl.BlockSpec(memory_space=pl.ANY)
    dma = pltpu.SemaphoreType.DMA
    return pl.pallas_call(
        functools.partial(fit_kernel, owners, cores, units, groups, tail),
        out_shape=(
            jax.ShapeDtypeStruct((units, PANELS, owners, PW, lanes), BF16),
            jax.ShapeDtypeStruct((units, eq_count, unit_cols), F32),
            jax.ShapeDtypeStruct((eq_count, WIDE), F32),
            jax.ShapeDtypeStruct((WIDE, WIDE), F32),
        ),
        in_specs=[vmem, vmem, vmem, hbm, vmem, vmem, vmem],
        out_specs=(hbm, hbm, vmem, vmem),
        scratch_shapes=[
            pltpu.VMEM((units, unit_cols, desc), BF16),
            pltpu.VMEM((WIDE, desc), BF16),
            pltpu.VMEM((1, WIDE), F32),
            pltpu.VMEM((2, owner.shape[0], LANES), F32),
            pltpu.VMEM((owners, 8, span), BF16),
            pltpu.VMEM((cores, owners, 8, span), BF16),
            pltpu.VMEM((env_count, desc), BF16),
            pltpu.VMEM((units, eq_count, unit_cols), F32),
            pltpu.VMEM((cores, eq_count // cores, WIDE), F32),
            pltpu.VMEM((owners, cores, eq_count // cores, WIDE), F32),
            pltpu.VMEM((units, owners, eq_count, lanes), BF16),
            pltpu.VMEM((units, owners, eq_count, lanes), BF16),
            pltpu.VMEM((units, PANELS, owners, PW, lanes), BF16),
            dma((units,)),
            dma((1 + PANELS, units)),
            dma,
            dma((2, cores)),
            dma((2,)),
            dma((owners,)),
            dma((owners,)),
            dma((cores, owners)),
            dma((cores, owners)),
            dma((owners,)),
            dma((owners,)),
            dma((cores, owners)),
            dma((cores, owners)),
            dma((units, owners)),
            dma((units, owners)),
            dma((units, PANELS, 2 + line)),
            dma((units, PANELS, 2 + line)),
        ],
        compiler_params=pltpu.CompilerParams(collective_id=0, has_side_effects=True),
    )(
        descriptors, owner.reshape(1, -1), struct.reshape(1, -1), points, scale.reshape(1, -1),
        row_weight.reshape(1, -1), ridge.reshape(1, 1),
    )


def place_of(owner, unit, owners):
    first, second = unit % 2, (unit + 1) % 2
    return (
        (owner >> first) % 2 * (owners // 2) + (owner >> second) % 2 * (owners // 4) + owner // 4
    )


def finish_kernel(norm_scale, coupled_ref, matrix_ref, q_ref, r_head_ref, r_ref, reduced_ref):
    units, _, owners, _, _ = coupled_ref.shape
    unit_cols = matrix_ref.shape[2]
    width = unit_cols // owners
    q_cols = q_ref[...]
    q_high, q_low = split_bf16(q_cols)
    q_wide = jnp.concatenate([q_high, q_low], axis=1)
    for u in range(units):
        coupled = jnp.concatenate(
            [
                jnp.concatenate(
                    [
                        coupled_ref[u, k, place_of(p, u, owners)][:, :width]
                        for p in range(owners)
                    ],
                    axis=1,
                )
                for k in range(PANELS)
            ],
            axis=0,
        )
        update = mm(q_wide, jnp.concatenate([coupled, coupled], axis=0), ((1,), (0,)), None)
        at = slice(u * unit_cols, (u + 1) * unit_cols)
        r_ref[:, at] = coupled.astype(F32) * norm_scale
        reduced_ref[:, at] = matrix_ref[u] - update

    @pl.when(lax.axis_index("cols") == 0)
    def _():
        r_ref[:, :WIDE] = r_head_ref[...] * norm_scale
        reduced_ref[:, :WIDE] = q_cols


def finish(coupled, matrix, q_cols, r_head, norm_scale):
    units = coupled.shape[0]
    _, eq_count, unit_cols = matrix.shape
    return pl.pallas_call(
        functools.partial(finish_kernel, norm_scale),
        out_shape=(
            jax.ShapeDtypeStruct((WIDE, units * unit_cols), F32),
            jax.ShapeDtypeStruct((eq_count, units * unit_cols), F32),
        ),
    )(coupled, matrix, q_cols, r_head)


def body(
    descriptors, sparse_points, point_scale, env_owner, env_structure, row_weight, ridge_factor
):
    owners, cores = lax.axis_size("rows"), lax.axis_size("cols")
    eq_count = row_weight.shape[0]
    env_local = descriptors.shape[0]
    col_count = sparse_points.shape[0]
    per_block = max(2, (3 * BLOCK + 2 * owners - 1) // (2 * owners))
    capacity = min(env_local, per_block * (-(-env_local // BLOCK)))
    units = max(1, min(UNITS, col_count // (LANES * owners)))
    coupled, matrix, q_cols, r_head = fit(
        descriptors, env_owner, env_structure, sparse_points, point_scale, row_weight,
        ridge_factor, owners, cores, units, capacity,
    )
    return finish(coupled, matrix, q_cols, r_head, 1.0 / math.sqrt(owners * eq_count))


def solution(mesh):
    return jax.shard_map(
        body,
        mesh=mesh,
        in_specs=(
            P(("rows", "cols"), None),
            P("cols", None),
            P("cols"),
            P("rows", None),
            P("rows"),
            P("rows"),
            P(),
        ),
        out_specs=(P(None, "cols"), P("rows", "cols")),
        check_vma=False,
    )
```

```python
import functools
import math

import jax
import jax.numpy as jnp
from jax import lax
from jax.experimental import pallas as pl
from jax.experimental.pallas import tpu as pltpu
from jax.sharding import PartitionSpec as P

PW = 64
PANELS = 2
WIDE = PW * PANELS
BLOCK = 128
LANES = 128
PIVOTS = 8
UNITS = 2
PARTS = 2
LAG = 0.9
HI = lax.Precision.HIGHEST
F32 = jnp.float32
BF16 = jnp.bfloat16
MESH = pl.DeviceIdType.MESH


def mm(left, right, contract, precision=HI):
    return lax.dot_general(
        left, right, ((contract[0], contract[1]), ((), ())), precision=precision,
        preferred_element_type=F32,
    )


def eliminate(system):
    rows = lax.broadcasted_iota(jnp.int32, (PW, WIDE), 0)
    for k in range(0, PW, PIVOTS):
        rest, index = system[k:], rows[k:]
        cols = [
            jnp.broadcast_to(rest[:, k + j:k + j + 1], rest.shape) for j in range(PIVOTS)
        ]
        tops = [rest[j:j + 1] for j in range(PIVOTS)]
        for p in range(PIVOTS):
            mult = jnp.where(index > k + p, cols[p] * (1.0 / cols[p][p:p + 1]), 0.0)
            for j in range(p + 1, PIVOTS):
                cols[j] = cols[j] - mult * cols[j][p:p + 1]
                tops[j] = tops[j] - mult[j:j + 1] * tops[p]
            cols[p] = mult
        for p in range(PIVOTS):
            rest = rest - cols[p] * tops[p]
        system = jnp.concatenate([system[:k], rest], axis=0) if k else rest
    return system


def factor(gram, ridge):
    row = lax.broadcasted_iota(jnp.int32, (PW, PW), 0)
    col = lax.broadcasted_iota(jnp.int32, (PW, PW), 1)
    on = row == col
    trace = jnp.sum(jnp.sum(jnp.where(on, gram, 0.0), axis=1, keepdims=True), axis=0, keepdims=True)
    shift = ridge * trace / PW + 1e-06
    eye = on.astype(F32)
    system = eliminate(jnp.concatenate([gram + shift * eye, eye], axis=1))
    left = system[:, :PW]
    diag = jnp.sum(jnp.where(on, left, 0.0), axis=1, keepdims=True)
    scale = lax.rsqrt(diag)
    upper = jnp.where(col >= row, left * scale, 0.0)
    return upper, system[:, PW:] * scale, shift


def bit_of(index, bit):
    return (index // (1 << bit)) % 2


def split_bf16(value):
    high = value.astype(BF16)
    return high, (value - high.astype(F32)).astype(BF16)


def fit_kernel(
    owners, cores, units, groups, tail,
    desc_ref, owner_ref, struct_ref, points_hbm, scale_ref, weight_ref, ridge_ref,
    coupled_hbm, matrix_hbm, q_ref, r_head_ref,
    points, head_points, head_scale, keys, parcel, landed, env, matrix,
    head_out, heads, block_out, block_in, whole,
    points_sem, out_sem, root_sem, root_send, root_recv, e_send, e_recv, f_send, f_recv,
    h_send, h_recv, k_send, k_recv, b_send, b_recv, r_send, r_recv,
):
    me = lax.axis_index("rows")
    core = lax.axis_index("cols")
    env_local, desc = desc_ref.shape
    eq_count = weight_ref.shape[1]
    col_count = scale_ref.shape[1]
    unit_cols = col_count // units
    width = unit_cols // owners
    lanes = block_in.shape[3]
    share = eq_count // cores
    line = owners // 4
    half_desc = desc // 2

    barrier = pltpu.get_barrier_semaphore()

    def greet_rows(d, _):
        pl.semaphore_signal(
            barrier, inc=1, device_id={"rows": (me + d) % owners}, device_id_type=MESH
        )
        return 0

    def greet_cols(d, _):
        pl.semaphore_signal(
            barrier, inc=1, device_id={"cols": (core + d) % cores}, device_id_type=MESH
        )
        return 0

    lax.fori_loop(1, owners, greet_rows, 0)
    lax.fori_loop(1, cores, greet_cols, 0)

    loads = []
    for u in range(units):
        load = pltpu.make_async_copy(
            points_hbm.at[pl.ds(u * unit_cols, unit_cols)], points.at[u], points_sem.at[u]
        )
        load.start()
        loads.append(load)

    def as_column(row):
        return jnp.broadcast_to(row.astype(F32), (LANES, row.shape[1])).T

    keys[0] = as_column(owner_ref[...])
    keys[1] = as_column(struct_ref[...])
    mine = pl.ds(pl.multiple_of(core * env_local, 8), env_local)
    own, struct = keys[0, mine], keys[1, mine]
    lane = lax.broadcasted_iota(jnp.int32, (env_local, LANES), 1).astype(F32)
    named = own == lane
    before = (
        lax.broadcasted_iota(jnp.int32, (env_local, env_local), 0)
        > lax.broadcasted_iota(jnp.int32, (env_local, env_local), 1)
    )
    ahead = mm(
        jnp.where(before, 1.0, 0.0).astype(BF16), jnp.where(named, 1.0, 0.0).astype(BF16),
        ((1,), (0,)), None,
    )
    within = jnp.sum(jnp.where(named, ahead, 0.0), axis=1, keepdims=True)
    own, struct = own[:, :1], struct[:, :1]
    place = lax.broadcasted_iota(jnp.int32, (env_local, owners * 8), 1).astype(F32)

    def pick(first, count, shift):
        inside = (within >= first) & (within < first + count)
        spot_of = jnp.where(inside, own * 8 + (within - first) + shift, -1.0)
        return jnp.where(place == spot_of, 1.0, 0.0).astype(BF16)

    descriptors = desc_ref[...]
    label = jnp.zeros((owners * 8, LANES), F32)
    for g in range(groups):
        chosen = pick(8 * g, 8, 0)
        block = mm(chosen, descriptors, ((0,), (0,)), None)
        parcel[:, :, g * desc:(g + 1) * desc] = block.reshape(owners, 8, desc).astype(BF16)
        tag = jnp.where(lane == g, struct + 1.0, 0.0).astype(BF16)
        label = label + mm(chosen, tag, ((0,), (0,)), None)
    edge = groups * desc
    if tail:
        lower, upper = pick(8 * groups, 4, 0), pick(8 * groups, 4, 4)
        block = mm(lower, descriptors[:, :half_desc], ((0,), (0,)), None) + mm(
            upper, descriptors[:, half_desc:], ((0,), (0,)), None
        )
        parcel[:, :, edge:edge + half_desc] = block.reshape(owners, 8, half_desc).astype(BF16)
        tag = jnp.where(lane == groups, struct + 1.0, 0.0).astype(BF16)
        label = label + mm(lower, tag, ((0,), (0,)), None)
        edge = edge + half_desc
    parcel[:, :, edge:] = label.reshape(owners, 8, LANES).astype(BF16)

    pl.semaphore_wait(barrier, owners + cores - 2)

    def exchange(src_of, slot_of, send, recv):
        def copy(to, sender):
            return pltpu.make_async_remote_copy(
                src_ref=src_of(to), dst_ref=slot_of(sender), send_sem=send.at[to],
                recv_sem=recv.at[sender], device_id={"rows": to}, device_id_type=MESH,
            )

        def start(d, _):
            copy((me + d) % owners, me).start()
            return 0

        def end(d, _):
            other = (me + d) % owners
            copy(other, other).wait_send()
            copy(other, other).wait_recv()
            return 0

        return start, end, copy

    start, _, routed = exchange(
        lambda to: parcel.at[to], lambda sender: landed.at[core, sender], e_send, e_recv
    )
    lax.fori_loop(1, owners, start, 0)

    def root_copies(to):
        pair = []
        for i, (src, dst) in enumerate(
            ((points_hbm.at[pl.ds(0, WIDE)], head_points), (scale_ref.at[:, pl.ds(0, WIDE)], head_scale))
        ):
            pair.append(
                pltpu.make_async_remote_copy(
                    src_ref=src, dst_ref=dst, send_sem=root_send.at[i, to],
                    recv_sem=root_recv.at[i], device_id={"cols": to}, device_id_type=MESH,
                )
            )
        return pair

    own_points = pltpu.make_async_copy(points_hbm.at[pl.ds(0, WIDE)], head_points, root_sem)

    @pl.when(core == 0)
    def _():
        own_points.start()
        head_scale[...] = scale_ref[:, :WIDE]
        for to in range(1, cores):
            for copy in root_copies(to):
                copy.start()

    def pass_on(slot, to, sender):
        return pltpu.make_async_remote_copy(
            src_ref=landed.at[sender, slot], dst_ref=landed.at[sender, slot],
            send_sem=f_send.at[to, slot], recv_sem=f_recv.at[sender, slot],
            device_id={"cols": to}, device_id_type=MESH,
        )

    def pass_all(slot):
        def one(d, _):
            pass_on(slot, (core + d) % cores, core).start()
            return 0

        lax.fori_loop(1, cores, one, 0)

    landed[core, me] = parcel[me]
    pass_all(me)

    def land(d, _):
        other = (me + d) % owners
        routed(other, other).wait_recv()
        pass_all(other)
        return 0

    lax.fori_loop(1, owners, land, 0)

    @pl.when(core == 0)
    def _():
        own_points.wait()
        for to in range(1, cores):
            for copy in root_copies(to):
                copy.wait_send()

    @pl.when(core != 0)
    def _():
        for copy in root_copies(0):
            copy.wait_recv()

    def passed(i, _):
        slot = i % owners
        other = (core + 1 + i // owners) % cores
        pass_on(slot, other, other).wait_recv()
        return 0

    lax.fori_loop(0, owners * (cores - 1), passed, 0)

    targets = lax.broadcasted_iota(jnp.int32, (1, LANES), 1).astype(F32)
    low_half = lax.broadcasted_iota(jnp.int32, (owners // 2, 8, 1), 1) < 4
    marks = []
    row = 0

    def swap(value):
        return jnp.concatenate([value[:, 4:], value[:, :4]], axis=1)

    def evens(value):
        paired = value.reshape((owners // 2, 2) + value.shape[1:])
        return paired[:, 0], paired[:, 1]

    for c in range(cores):
        tags = landed[c, :, :, edge:].astype(F32)
        for g in range(groups):
            env[row:row + owners * 8] = landed[c, :, :, g * desc:(g + 1) * desc].astype(
                F32
            ).reshape(owners * 8, desc).astype(BF16)
            tag = tags[:, :, g:g + 1].reshape(owners * 8, 1) - 1.0
            marks.append(jnp.where(tag == targets, 1.0, 0.0))
            row += owners * 8
        if tail:
            first, second = evens(
                landed[c, :, :, groups * desc:groups * desc + half_desc].astype(F32)
            )
            left = jnp.where(low_half, first, swap(second))
            right = jnp.where(low_half, swap(first), second)
            env[row:row + owners * 4, :half_desc] = left.reshape(owners * 4, half_desc).astype(BF16)
            env[row:row + owners * 4, half_desc:] = right.reshape(owners * 4, half_desc).astype(BF16)
            first, second = evens(jnp.broadcast_to(tags[:, :, groups:groups + 1], tags.shape))
            tag = jnp.where(low_half, first, swap(second)).reshape(owners * 4, LANES) - 1.0
            marks.append(jnp.where(tag == targets, 1.0, 0.0))
            row += owners * 4
    selector = jnp.concatenate(marks, axis=0).T[:eq_count].astype(BF16)
    weight = as_column(weight_ref[...])[:, :1]

    def equations(rows, scale):
        products = mm(env[...], rows, ((1,), (1,)), None) * desc ** (-0.5)
        squared = products * products
        kernel = (scale * squared * squared).astype(BF16)
        return mm(selector, kernel, ((1,), (0,)), None) * weight

    head = equations(head_points[...], head_scale[...])
    for c in range(cores):
        head_out[c] = head[c * share:(c + 1) * share].astype(BF16)
    start, _, shared = exchange(
        lambda to: head_out.at[core], lambda sender: heads.at[sender, core], h_send, h_recv
    )
    lax.fori_loop(1, owners, start, 0)
    heads[me] = head_out[...]

    outs = []
    blocks = []
    for u in range(units):
        loads[u].wait()
        value = equations(points[u], scale_ref[:, u * unit_cols:(u + 1) * unit_cols])
        matrix[u] = value
        out = pltpu.make_async_copy(matrix.at[u], matrix_hbm.at[u], out_sem.at[0, u])
        out.start()
        outs.append(out)
        value = value.astype(BF16)
        for p in range(owners):
            block_out[u, p, :, :width] = value[:, p * width:(p + 1) * width]
        start, end, _ = exchange(
            lambda to, u=u: block_out.at[u, to], lambda sender, u=u: block_in.at[u, sender],
            b_send.at[u], b_recv.at[u],
        )
        lax.fori_loop(1, owners, start, 0)
        block_in[u, me] = block_out[u, me]
        blocks.append(end)

    def hand_head(slot, to, sender):
        part = heads.at[slot, sender]
        return pltpu.make_async_remote_copy(
            src_ref=part, dst_ref=part, send_sem=k_send.at[to, slot],
            recv_sem=k_recv.at[sender, slot], device_id={"cols": to}, device_id_type=MESH,
        )

    def land_head(d, _):
        other = (me + d) % owners
        shared(other, other).wait_recv()

        def one(e, _):
            hand_head(other, (core + e) % cores, core).start()
            return 0

        lax.fori_loop(1, cores, one, 0)
        return 0

    lax.fori_loop(1, owners, land_head, 0)

    def handed(i, _):
        other = (core + 1 + i // (owners - 1)) % cores
        hand_head((me + 1 + i % (owners - 1)) % owners, other, other).wait_recv()
        return 0

    lax.fori_loop(0, (owners - 1) * (cores - 1), handed, 0)

    every = heads[...].astype(F32).reshape(owners * eq_count, WIDE).T.astype(BF16)
    gram = mm(every, every, ((1,), (1,)), None)
    ridge = ridge_ref[...]
    up1, inv1, shift = factor(gram[:PW, :PW], ridge)
    c12 = mm(inv1, gram[:PW, PW:], ((1,), (0,)))
    back = mm(inv1, c12, ((0,), (0,)))
    pair = jnp.concatenate([c12, jnp.sqrt(shift) * back], axis=0)
    deep = c12 + shift * mm(inv1, back, ((1,), (0,)))
    up2, inv2, _ = factor(gram[PW:, PW:] - mm(pair, pair, ((0,), (0,))), ridge)
    q1 = mm(head[:, :PW], inv1, ((1,), (1,)))
    q2 = mm(head[:, PW:] - mm(q1, c12, ((1,), (0,))), inv2, ((1,), (1,)))
    q_ref[...] = jnp.concatenate([q1, q2], axis=1)
    r_head_ref[...] = jnp.concatenate(
        [
            jnp.concatenate([up1, c12], axis=1),
            jnp.concatenate([jnp.zeros((PW, PW), F32), up2], axis=1),
        ],
        axis=0,
    )

    rank = me // 4

    def bit(u, t):
        return (t + u) % 2

    def start_of(u, t):
        return sum(
            (bit_of(me, bit(u, i)) * (owners >> (i + 1)) for i in range(t)), jnp.int32(0)
        )

    def quarter_copy(u, k, t, second):
        quarter = owners // 4
        own = bit_of(me, bit(u, 1))
        at = start_of(u, 1) + (1 - own if second else own) * quarter
        part = whole.at[u, k, pl.ds(at, quarter)]
        to = me + (1 - 2 * bit_of(me, bit(u, t))) * (1 << bit(u, t))
        index = 2 * t + second
        return pltpu.make_async_remote_copy(
            src_ref=part, dst_ref=part, send_sem=r_send.at[u, k, index],
            recv_sem=r_recv.at[u, k, index], device_id={"rows": to}, device_id_type=MESH,
        )

    def gather_copy(u, k, index):
        return quarter_copy(u, k, (0, 0, 1)[index], (False, True, False)[index])

    def line_copy(u, k, to, sender):
        part = whole.at[u, k, start_of(u, 2) + sender]
        return pltpu.make_async_remote_copy(
            src_ref=part, dst_ref=part, send_sem=r_send.at[u, k, 3 + to],
            recv_sem=r_recv.at[u, k, 3 + sender],
            device_id={"rows": to * 4 + me % 4}, device_id_type=MESH,
        )

    others = [(rank + d) % line for d in range(1, line)]

    def open_piece(u, k, value):
        whole[u, k, start_of(u, 2) + rank] = value.astype(BF16)
        for to in others:
            line_copy(u, k, to, rank).start()

    def open_unit(u):
        lax.fori_loop(1, owners, blocks[u], 0)
        block = block_in[u].astype(F32).reshape(owners * eq_count, lanes).astype(BF16)
        cross = mm(every, block, ((1,), (0,)), None)
        first = mm(inv1, cross[:PW], ((1,), (0,)))
        open_piece(u, 0, first)
        rest = cross[PW:] - mm(deep, first, ((0,), (0,)))
        open_piece(u, 1, mm(inv2, rest, ((1,), (0,))))

    def line_end(u):
        for k in range(PANELS):
            for other in others:
                line_copy(u, k, other, other).wait_recv()
            gather_copy(u, k, 2).start()
            gather_copy(u, k, 0).start()

    def middle(u):
        for k in range(PANELS):
            gather_copy(u, k, 2).wait_recv()
            gather_copy(u, k, 1).start()

    def last(u):
        for k in range(PANELS):
            gather_copy(u, k, 0).wait_recv()
            gather_copy(u, k, 1).wait_recv()
        out = pltpu.make_async_copy(whole.at[u], coupled_hbm.at[u], out_sem.at[1, u])
        out.start()
        outs.append(out)

    steps = (open_unit, line_end, middle, last)
    plan = sorted((s + LAG * u, u, s) for u in range(units) for s in range(len(steps)))
    for _, u, s in plan:
        steps[s](u)

    for u in range(units):
        for k in range(PANELS):
            for index in range(3):
                gather_copy(u, k, index).wait_send()
            for to in others:
                line_copy(u, k, to, rank).wait_send()
    for out in outs:
        out.wait()

    def drain(d, _):
        other = (me + d) % owners
        routed(other, other).wait_send()
        shared(other, other).wait_send()
        return 0

    lax.fori_loop(1, owners, drain, 0)

    def drain_pass(i, _):
        pass_on(i % owners, (core + 1 + i // owners) % cores, core).wait_send()
        return 0

    lax.fori_loop(0, owners * (cores - 1), drain_pass, 0)

    def drain_head(i, _):
        to = (core + 1 + i // (owners - 1)) % cores
        hand_head((me + 1 + i % (owners - 1)) % owners, to, core).wait_send()
        return 0

    lax.fori_loop(0, (owners - 1) * (cores - 1), drain_head, 0)


def fit(descriptors, owner, struct, points, scale, row_weight, ridge, owners, cores, units, capacity):
    col_count, desc = points.shape
    unit_cols = col_count // units
    eq_count = row_weight.shape[0]
    lanes = max(LANES, unit_cols // owners)
    left = capacity % 8
    tail = 0 < left <= 4
    groups = capacity // 8 + (left > 4)
    span = groups * desc + (desc // 2 if tail else 0) + LANES
    env_count = cores * owners * (8 * groups + 4 * tail)
    line = owners // 4
    vmem = pl.BlockSpec(memory_space=pltpu.VMEM)
    hbm = pl.BlockSpec(memory_space=pl.ANY)
    dma = pltpu.SemaphoreType.DMA
    return pl.pallas_call(
        functools.partial(fit_kernel, owners, cores, units, groups, tail),
        out_shape=(
            jax.ShapeDtypeStruct((units, PANELS, owners, PW, lanes), BF16),
            jax.ShapeDtypeStruct((units, eq_count, unit_cols), F32),
            jax.ShapeDtypeStruct((eq_count, WIDE), F32),
            jax.ShapeDtypeStruct((WIDE, WIDE), F32),
        ),
        in_specs=[vmem, vmem, vmem, hbm, vmem, vmem, vmem],
        out_specs=(hbm, hbm, vmem, vmem),
        scratch_shapes=[
            pltpu.VMEM((units, unit_cols, desc), BF16),
            pltpu.VMEM((WIDE, desc), BF16),
            pltpu.VMEM((1, WIDE), F32),
            pltpu.VMEM((2, owner.shape[0], LANES), F32),
            pltpu.VMEM((owners, 8, span), BF16),
            pltpu.VMEM((cores, owners, 8, span), BF16),
            pltpu.VMEM((env_count, desc), BF16),
            pltpu.VMEM((units, eq_count, unit_cols), F32),
            pltpu.VMEM((cores, eq_count // cores, WIDE), BF16),
            pltpu.VMEM((owners, cores, eq_count // cores, WIDE), BF16),
            pltpu.VMEM((units, owners, eq_count, lanes), BF16),
            pltpu.VMEM((units, owners, eq_count, lanes), BF16),
            pltpu.VMEM((units, PANELS, owners, PW, lanes), BF16),
            dma((units,)),
            dma((2, units)),
            dma,
            dma((2, cores)),
            dma((2,)),
            dma((owners,)),
            dma((owners,)),
            dma((cores, owners)),
            dma((cores, owners)),
            dma((owners,)),
            dma((owners,)),
            dma((cores, owners)),
            dma((cores, owners)),
            dma((units, owners)),
            dma((units, owners)),
            dma((units, PANELS, 3 + line)),
            dma((units, PANELS, 3 + line)),
        ],
        compiler_params=pltpu.CompilerParams(collective_id=0, has_side_effects=True),
    )(
        descriptors, owner.reshape(1, -1), struct.reshape(1, -1), points, scale.reshape(1, -1),
        row_weight.reshape(1, -1), ridge.reshape(1, 1),
    )


def place_of(owner, unit, owners):
    first, second = unit % 2, (unit + 1) % 2
    return (
        (owner >> first) % 2 * (owners // 2) + (owner >> second) % 2 * (owners // 4) + owner // 4
    )


def finish_kernel(
    norm_scale, coupled_hbm, matrix_hbm, q_ref, r_head_ref, r_hbm, reduced_hbm,
    coupled, matrix, r_out, reduced_out, in_sem, out_sem,
):
    units, _, owners, _, _ = coupled.shape
    unit_cols = matrix.shape[2]
    width = unit_cols // owners
    loads = []
    for u in range(units):
        pair = (
            pltpu.make_async_copy(coupled_hbm.at[u], coupled.at[u], in_sem.at[0, u]),
            pltpu.make_async_copy(matrix_hbm.at[u], matrix.at[u], in_sem.at[1, u]),
        )
        for load in pair:
            load.start()
        loads.append(pair)
    q_cols = q_ref[...]
    q_high, q_low = split_bf16(q_cols)
    q_wide = jnp.concatenate([q_high, q_low], axis=1)
    root = lax.axis_index("cols") == 0
    part = unit_cols // PARTS
    stores = []
    for u in range(units):
        for load in loads[u]:
            load.wait()
        for h in range(PARTS):
            mine = range(h * owners // PARTS, (h + 1) * owners // PARTS)
            block = jnp.concatenate(
                [
                    jnp.concatenate(
                        [coupled[u, k, place_of(p, u, owners)][:, :width] for p in mine], axis=1
                    )
                    for k in range(PANELS)
                ],
                axis=0,
            )
            update = mm(q_wide, jnp.concatenate([block, block], axis=0), ((1,), (0,)), None)
            at = slice(u * unit_cols + h * part, u * unit_cols + (h + 1) * part)
            r_out[:, at] = block.astype(F32) * norm_scale
            reduced_out[:, at] = matrix[u, :, h * part:(h + 1) * part] - update
            if u == 0 and h == 0:
                r_out[:, :WIDE] = jnp.where(root, r_head_ref[...] * norm_scale, r_out[:, :WIDE])
                reduced_out[:, :WIDE] = jnp.where(root, q_cols, reduced_out[:, :WIDE])
            for i, (src, dst) in enumerate(((r_out, r_hbm), (reduced_out, reduced_hbm))):
                store = pltpu.make_async_copy(
                    src.at[:, at], dst.at[:, at], out_sem.at[i, u * PARTS + h]
                )
                store.start()
                stores.append(store)
    for store in stores:
        store.wait()


def finish(coupled, matrix, q_cols, r_head, norm_scale):
    units = coupled.shape[0]
    _, eq_count, unit_cols = matrix.shape
    vmem = pl.BlockSpec(memory_space=pltpu.VMEM)
    hbm = pl.BlockSpec(memory_space=pl.ANY)
    r_shape = (WIDE, units * unit_cols)
    reduced_shape = (eq_count, units * unit_cols)
    return pl.pallas_call(
        functools.partial(finish_kernel, norm_scale),
        out_shape=(
            jax.ShapeDtypeStruct(r_shape, F32),
            jax.ShapeDtypeStruct(reduced_shape, F32),
        ),
        in_specs=[hbm, hbm, vmem, vmem],
        out_specs=(hbm, hbm),
        scratch_shapes=[
            pltpu.VMEM(coupled.shape, BF16),
            pltpu.VMEM(matrix.shape, F32),
            pltpu.VMEM(r_shape, F32),
            pltpu.VMEM(reduced_shape, F32),
            pltpu.SemaphoreType.DMA((2, units)),
            pltpu.SemaphoreType.DMA((2, units * PARTS)),
        ],
    )(coupled, matrix, q_cols, r_head)


def body(
    descriptors, sparse_points, point_scale, env_owner, env_structure, row_weight, ridge_factor
):
    owners, cores = lax.axis_size("rows"), lax.axis_size("cols")
    eq_count = row_weight.shape[0]
    env_local = descriptors.shape[0]
    col_count = sparse_points.shape[0]
    per_block = max(2, (3 * BLOCK + 2 * owners - 1) // (2 * owners))
    capacity = min(env_local, per_block * (-(-env_local // BLOCK)))
    units = max(1, min(UNITS, col_count // (LANES * owners)))
    coupled, matrix, q_cols, r_head = fit(
        descriptors, env_owner, env_structure, sparse_points, point_scale, row_weight,
        ridge_factor, owners, cores, units, capacity,
    )
    return finish(coupled, matrix, q_cols, r_head, 1.0 / math.sqrt(owners * eq_count))


def solution(mesh):
    return jax.shard_map(
        body,
        mesh=mesh,
        in_specs=(
            P(("rows", "cols"), None),
            P("cols", None),
            P("cols"),
            P("rows", None),
            P("rows"),
            P("rows"),
            P(),
        ),
        out_specs=(P(None, "cols"), P("rows", "cols")),
        check_vma=False,
    )
```

```python
import functools
import math

import jax
import jax.numpy as jnp
from jax import lax
from jax.experimental import pallas as pl
from jax.experimental.pallas import tpu as pltpu
from jax.sharding import PartitionSpec as P

PW = 64
PANELS = 2
WIDE = PW * PANELS
BLOCK = 128
LANES = 128
PIVOTS = 8
UNITS = 2
PARTS = 2
LAG = 0.9
FIT_VMEM = 44 << 20
FINISH_VMEM = 16 << 20
HI = lax.Precision.HIGHEST
F32 = jnp.float32
BF16 = jnp.bfloat16
MESH = pl.DeviceIdType.MESH


def mm(left, right, contract, precision=HI):
    return lax.dot_general(
        left, right, ((contract[0], contract[1]), ((), ())), precision=precision,
        preferred_element_type=F32,
    )


def eliminate(system):
    rows = lax.broadcasted_iota(jnp.int32, (PW, WIDE), 0)
    for k in range(0, PW, PIVOTS):
        rest, index = system[k:], rows[k:]
        cols = [
            jnp.broadcast_to(rest[:, k + j:k + j + 1], rest.shape) for j in range(PIVOTS)
        ]
        tops = [rest[j:j + 1] for j in range(PIVOTS)]
        for p in range(PIVOTS):
            mult = jnp.where(index > k + p, cols[p] * (1.0 / cols[p][p:p + 1]), 0.0)
            for j in range(p + 1, PIVOTS):
                cols[j] = cols[j] - mult * cols[j][p:p + 1]
                tops[j] = tops[j] - mult[j:j + 1] * tops[p]
            cols[p] = mult
        for p in range(PIVOTS):
            rest = rest - cols[p] * tops[p]
        system = jnp.concatenate([system[:k], rest], axis=0) if k else rest
    return system


def factor(gram, ridge):
    row = lax.broadcasted_iota(jnp.int32, (PW, PW), 0)
    col = lax.broadcasted_iota(jnp.int32, (PW, PW), 1)
    on = row == col
    trace = jnp.sum(jnp.sum(jnp.where(on, gram, 0.0), axis=1, keepdims=True), axis=0, keepdims=True)
    shift = ridge * trace / PW + 1e-06
    eye = on.astype(F32)
    system = eliminate(jnp.concatenate([gram + shift * eye, eye], axis=1))
    left = system[:, :PW]
    diag = jnp.sum(jnp.where(on, left, 0.0), axis=1, keepdims=True)
    scale = lax.rsqrt(diag)
    upper = jnp.where(col >= row, left * scale, 0.0)
    return upper, system[:, PW:] * scale, shift


def bit_of(index, bit):
    return (index // (1 << bit)) % 2


def split_bf16(value):
    high = value.astype(BF16)
    return high, (value - high.astype(F32)).astype(BF16)


def fit_kernel(
    owners, cores, units, groups, tail,
    desc_hbm, owner_hbm, struct_hbm, points_hbm, scale_hbm, weight_hbm, ridge_hbm,
    coupled_ref, matrix_ref, q_ref, r_head_ref,
    desc_ref, owner_ref, struct_ref, scale_ref, weight_ref, ridge_ref,
    points, head_points, head_scale, keys, parcel, landed, env,
    head_out, heads, block_out, block_in, whole,
    start_sem, points_sem, out_sem, root_sem, root_send, root_recv, e_send, e_recv, f_send, f_recv,
    h_send, h_recv, k_send, k_recv, b_send, b_recv, r_send, r_recv,
):
    me = lax.axis_index("rows")
    core = lax.axis_index("cols")
    env_local, desc = desc_ref.shape
    eq_count = weight_ref.shape[1]
    col_count = scale_ref.shape[1]
    unit_cols = col_count // units
    width = unit_cols // owners
    lanes = block_in.shape[3]
    share = eq_count // cores
    line = owners // 4
    half_desc = desc // 2

    barrier = pltpu.get_barrier_semaphore()

    def greet_rows(d, _):
        pl.semaphore_signal(
            barrier, inc=1, device_id={"rows": (me + d) % owners}, device_id_type=MESH
        )
        return 0

    def greet_cols(d, _):
        pl.semaphore_signal(
            barrier, inc=1, device_id={"cols": (core + d) % cores}, device_id_type=MESH
        )
        return 0

    lax.fori_loop(1, owners, greet_rows, 0)
    lax.fori_loop(1, cores, greet_cols, 0)

    inputs = (
        (owner_hbm, owner_ref), (struct_hbm, struct_ref), (desc_hbm, desc_ref),
        (scale_hbm, scale_ref), (weight_hbm, weight_ref), (ridge_hbm, ridge_ref),
    )
    inputs = [
        pltpu.make_async_copy(src, dst, start_sem.at[i]) for i, (src, dst) in enumerate(inputs)
    ]
    for load in inputs:
        load.start()
    loads = []
    for u in range(units):
        load = pltpu.make_async_copy(
            points_hbm.at[pl.ds(u * unit_cols, unit_cols)], points.at[u], points_sem.at[u]
        )
        load.start()
        loads.append(load)

    def as_column(row):
        return jnp.broadcast_to(row.astype(F32), (LANES, row.shape[1])).T

    for load in inputs:
        load.wait()
    keys[0] = as_column(owner_ref[...])
    keys[1] = as_column(struct_ref[...])
    mine = pl.ds(pl.multiple_of(core * env_local, 8), env_local)
    own, struct = keys[0, mine], keys[1, mine]
    lane = lax.broadcasted_iota(jnp.int32, (env_local, LANES), 1).astype(F32)
    named = own == lane
    before = (
        lax.broadcasted_iota(jnp.int32, (env_local, env_local), 0)
        > lax.broadcasted_iota(jnp.int32, (env_local, env_local), 1)
    )
    ahead = mm(
        jnp.where(before, 1.0, 0.0).astype(BF16), jnp.where(named, 1.0, 0.0).astype(BF16),
        ((1,), (0,)), None,
    )
    within = jnp.sum(jnp.where(named, ahead, 0.0), axis=1, keepdims=True)
    own, struct = own[:, :1], struct[:, :1]
    place = lax.broadcasted_iota(jnp.int32, (env_local, owners * 8), 1).astype(F32)

    def pick(first, count, shift):
        inside = (within >= first) & (within < first + count)
        spot_of = jnp.where(inside, own * 8 + (within - first) + shift, -1.0)
        return jnp.where(place == spot_of, 1.0, 0.0).astype(BF16)

    descriptors = desc_ref[...]
    label = jnp.zeros((owners * 8, LANES), F32)
    for g in range(groups):
        chosen = pick(8 * g, 8, 0)
        block = mm(chosen, descriptors, ((0,), (0,)), None)
        parcel[:, :, g * desc:(g + 1) * desc] = block.reshape(owners, 8, desc).astype(BF16)
        tag = jnp.where(lane == g, struct + 1.0, 0.0).astype(BF16)
        label = label + mm(chosen, tag, ((0,), (0,)), None)
    edge = groups * desc
    if tail:
        lower, upper = pick(8 * groups, 4, 0), pick(8 * groups, 4, 4)
        block = mm(lower, descriptors[:, :half_desc], ((0,), (0,)), None) + mm(
            upper, descriptors[:, half_desc:], ((0,), (0,)), None
        )
        parcel[:, :, edge:edge + half_desc] = block.reshape(owners, 8, half_desc).astype(BF16)
        tag = jnp.where(lane == groups, struct + 1.0, 0.0).astype(BF16)
        label = label + mm(lower, tag, ((0,), (0,)), None)
        edge = edge + half_desc
    parcel[:, :, edge:] = label.reshape(owners, 8, LANES).astype(BF16)

    pl.semaphore_wait(barrier, owners + cores - 2)

    def exchange(src_of, slot_of, send, recv):
        def copy(to, sender):
            return pltpu.make_async_remote_copy(
                src_ref=src_of(to), dst_ref=slot_of(sender), send_sem=send.at[to],
                recv_sem=recv.at[sender], device_id={"rows": to}, device_id_type=MESH,
            )

        def start(d, _):
            copy((me + d) % owners, me).start()
            return 0

        def end(d, _):
            other = (me + d) % owners
            copy(other, other).wait_send()
            copy(other, other).wait_recv()
            return 0

        return start, end, copy

    start, _, routed = exchange(
        lambda to: parcel.at[to], lambda sender: landed.at[core, sender], e_send, e_recv
    )
    lax.fori_loop(1, owners, start, 0)

    def root_copies(to):
        pair = []
        for i, (src, dst) in enumerate(
            ((points_hbm.at[pl.ds(0, WIDE)], head_points), (scale_ref.at[:, pl.ds(0, WIDE)], head_scale))
        ):
            pair.append(
                pltpu.make_async_remote_copy(
                    src_ref=src, dst_ref=dst, send_sem=root_send.at[i, to],
                    recv_sem=root_recv.at[i], device_id={"cols": to}, device_id_type=MESH,
                )
            )
        return pair

    own_points = pltpu.make_async_copy(points_hbm.at[pl.ds(0, WIDE)], head_points, root_sem)

    @pl.when(core == 0)
    def _():
        own_points.start()
        head_scale[...] = scale_ref[:, :WIDE]
        for to in range(1, cores):
            for copy in root_copies(to):
                copy.start()

    def pass_on(slot, to, sender):
        return pltpu.make_async_remote_copy(
            src_ref=landed.at[sender, slot], dst_ref=landed.at[sender, slot],
            send_sem=f_send.at[to, slot], recv_sem=f_recv.at[sender, slot],
            device_id={"cols": to}, device_id_type=MESH,
        )

    def pass_all(slot):
        def one(d, _):
            pass_on(slot, (core + d) % cores, core).start()
            return 0

        lax.fori_loop(1, cores, one, 0)

    landed[core, me] = parcel[me]
    pass_all(me)

    def land(d, _):
        other = (me + d) % owners
        routed(other, other).wait_recv()
        pass_all(other)
        return 0

    lax.fori_loop(1, owners, land, 0)

    @pl.when(core == 0)
    def _():
        own_points.wait()
        for to in range(1, cores):
            for copy in root_copies(to):
                copy.wait_send()

    @pl.when(core != 0)
    def _():
        for copy in root_copies(0):
            copy.wait_recv()

    def passed(i, _):
        slot = i % owners
        other = (core + 1 + i // owners) % cores
        pass_on(slot, other, other).wait_recv()
        return 0

    lax.fori_loop(0, owners * (cores - 1), passed, 0)

    targets = lax.broadcasted_iota(jnp.int32, (1, LANES), 1).astype(F32)
    low_half = lax.broadcasted_iota(jnp.int32, (owners // 2, 8, 1), 1) < 4
    marks = []
    row = 0

    def swap(value):
        return jnp.concatenate([value[:, 4:], value[:, :4]], axis=1)

    def evens(value):
        paired = value.reshape((owners // 2, 2) + value.shape[1:])
        return paired[:, 0], paired[:, 1]

    for c in range(cores):
        tags = landed[c, :, :, edge:].astype(F32)
        for g in range(groups):
            env[row:row + owners * 8] = landed[c, :, :, g * desc:(g + 1) * desc].astype(
                F32
            ).reshape(owners * 8, desc).astype(BF16)
            tag = tags[:, :, g:g + 1].reshape(owners * 8, 1) - 1.0
            marks.append(jnp.where(tag == targets, 1.0, 0.0))
            row += owners * 8
        if tail:
            first, second = evens(
                landed[c, :, :, groups * desc:groups * desc + half_desc].astype(F32)
            )
            left = jnp.where(low_half, first, swap(second))
            right = jnp.where(low_half, swap(first), second)
            env[row:row + owners * 4, :half_desc] = left.reshape(owners * 4, half_desc).astype(BF16)
            env[row:row + owners * 4, half_desc:] = right.reshape(owners * 4, half_desc).astype(BF16)
            first, second = evens(jnp.broadcast_to(tags[:, :, groups:groups + 1], tags.shape))
            tag = jnp.where(low_half, first, swap(second)).reshape(owners * 4, LANES) - 1.0
            marks.append(jnp.where(tag == targets, 1.0, 0.0))
            row += owners * 4
    selector = jnp.concatenate(marks, axis=0).T[:eq_count].astype(BF16)
    weight = as_column(weight_ref[...])[:, :1]

    def equations(rows, scale):
        products = mm(env[...], rows, ((1,), (1,)), None) * desc ** (-0.5)
        squared = products * products
        kernel = (scale * squared * squared).astype(BF16)
        return mm(selector, kernel, ((1,), (0,)), None) * weight

    head = equations(head_points[...], head_scale[...])
    for c in range(cores):
        head_out[c] = head[c * share:(c + 1) * share].astype(BF16)
    start, _, shared = exchange(
        lambda to: head_out.at[core], lambda sender: heads.at[sender, core], h_send, h_recv
    )
    lax.fori_loop(1, owners, start, 0)
    heads[me] = head_out[...]

    outs = []
    blocks = []
    for u in range(units):
        loads[u].wait()
        value = equations(points[u], scale_ref[:, u * unit_cols:(u + 1) * unit_cols])
        matrix_ref[u] = value
        value = value.astype(BF16)
        for p in range(owners):
            block_out[u, p, :, :width] = value[:, p * width:(p + 1) * width]
        start, end, _ = exchange(
            lambda to, u=u: block_out.at[u, to], lambda sender, u=u: block_in.at[u, sender],
            b_send.at[u], b_recv.at[u],
        )
        lax.fori_loop(1, owners, start, 0)
        block_in[u, me] = block_out[u, me]
        blocks.append(end)

    def hand_head(slot, to, sender):
        part = heads.at[slot, sender]
        return pltpu.make_async_remote_copy(
            src_ref=part, dst_ref=part, send_sem=k_send.at[to, slot],
            recv_sem=k_recv.at[sender, slot], device_id={"cols": to}, device_id_type=MESH,
        )

    def land_head(d, _):
        other = (me + d) % owners
        shared(other, other).wait_recv()

        def one(e, _):
            hand_head(other, (core + e) % cores, core).start()
            return 0

        lax.fori_loop(1, cores, one, 0)
        return 0

    lax.fori_loop(1, owners, land_head, 0)

    def handed(i, _):
        other = (core + 1 + i // (owners - 1)) % cores
        hand_head((me + 1 + i % (owners - 1)) % owners, other, other).wait_recv()
        return 0

    lax.fori_loop(0, (owners - 1) * (cores - 1), handed, 0)

    every = heads[...].astype(F32).reshape(owners * eq_count, WIDE).T.astype(BF16)
    gram = mm(every, every, ((1,), (1,)), None)
    ridge = ridge_ref[:, :1]
    up1, inv1, shift = factor(gram[:PW, :PW], ridge)
    c12 = mm(inv1, gram[:PW, PW:], ((1,), (0,)))
    back = mm(inv1, c12, ((0,), (0,)))
    pair = jnp.concatenate([c12, jnp.sqrt(shift) * back], axis=0)
    deep = c12 + shift * mm(inv1, back, ((1,), (0,)))
    up2, inv2, _ = factor(gram[PW:, PW:] - mm(pair, pair, ((0,), (0,))), ridge)
    q1 = mm(head[:, :PW], inv1, ((1,), (1,)))
    q2 = mm(head[:, PW:] - mm(q1, c12, ((1,), (0,))), inv2, ((1,), (1,)))
    q_ref[...] = jnp.concatenate([q1, q2], axis=1)
    r_head_ref[...] = jnp.concatenate(
        [
            jnp.concatenate([up1, c12], axis=1),
            jnp.concatenate([jnp.zeros((PW, PW), F32), up2], axis=1),
        ],
        axis=0,
    )

    rank = me // 4

    def bit(u, t):
        return (t + u) % 2

    def start_of(u, t):
        return sum(
            (bit_of(me, bit(u, i)) * (owners >> (i + 1)) for i in range(t)), jnp.int32(0)
        )

    def quarter_copy(u, k, t, second):
        quarter = owners // 4
        own = bit_of(me, bit(u, 1))
        at = start_of(u, 1) + (1 - own if second else own) * quarter
        part = whole.at[u, k, pl.ds(at, quarter)]
        to = me + (1 - 2 * bit_of(me, bit(u, t))) * (1 << bit(u, t))
        index = 2 * t + second
        return pltpu.make_async_remote_copy(
            src_ref=part, dst_ref=part, send_sem=r_send.at[u, k, index],
            recv_sem=r_recv.at[u, k, index], device_id={"rows": to}, device_id_type=MESH,
        )

    def gather_copy(u, k, index):
        return quarter_copy(u, k, (0, 0, 1)[index], (False, True, False)[index])

    def line_copy(u, k, to, sender):
        part = whole.at[u, k, start_of(u, 2) + sender]
        return pltpu.make_async_remote_copy(
            src_ref=part, dst_ref=part, send_sem=r_send.at[u, k, 3 + to],
            recv_sem=r_recv.at[u, k, 3 + sender],
            device_id={"rows": to * 4 + me % 4}, device_id_type=MESH,
        )

    others = [(rank + d) % line for d in range(1, line)]

    def open_piece(u, k, value):
        whole[u, k, start_of(u, 2) + rank] = value.astype(BF16)
        for to in others:
            line_copy(u, k, to, rank).start()

    def open_unit(u):
        lax.fori_loop(1, owners, blocks[u], 0)
        block = block_in[u].astype(F32).reshape(owners * eq_count, lanes).astype(BF16)
        cross = mm(every, block, ((1,), (0,)), None)
        first = mm(inv1, cross[:PW], ((1,), (0,)))
        open_piece(u, 0, first)
        rest = cross[PW:] - mm(deep, first, ((0,), (0,)))
        open_piece(u, 1, mm(inv2, rest, ((1,), (0,))))

    def line_end(u):
        for k in range(PANELS):
            for other in others:
                line_copy(u, k, other, other).wait_recv()
            gather_copy(u, k, 2).start()
            gather_copy(u, k, 0).start()

    def middle(u):
        for k in range(PANELS):
            gather_copy(u, k, 2).wait_recv()
            gather_copy(u, k, 1).start()

    def last(u):
        for k in range(PANELS):
            gather_copy(u, k, 0).wait_recv()
            gather_copy(u, k, 1).wait_recv()
        out = pltpu.make_async_copy(whole.at[u], coupled_ref.at[u], out_sem.at[u])
        out.start()
        outs.append(out)

    steps = (open_unit, line_end, middle, last)
    plan = sorted((s + LAG * u, u, s) for u in range(units) for s in range(len(steps)))
    for _, u, s in plan:
        steps[s](u)

    for u in range(units):
        for k in range(PANELS):
            for index in range(3):
                gather_copy(u, k, index).wait_send()
            for to in others:
                line_copy(u, k, to, rank).wait_send()
    for out in outs:
        out.wait()

    def drain(d, _):
        other = (me + d) % owners
        routed(other, other).wait_send()
        shared(other, other).wait_send()
        return 0

    lax.fori_loop(1, owners, drain, 0)

    def drain_pass(i, _):
        pass_on(i % owners, (core + 1 + i // owners) % cores, core).wait_send()
        return 0

    lax.fori_loop(0, owners * (cores - 1), drain_pass, 0)

    def drain_head(i, _):
        to = (core + 1 + i // (owners - 1)) % cores
        hand_head((me + 1 + i % (owners - 1)) % owners, to, core).wait_send()
        return 0

    lax.fori_loop(0, (owners - 1) * (cores - 1), drain_head, 0)


def fit(descriptors, owner, struct, points, scale, row_weight, ridge, owners, cores, units, capacity):
    col_count, desc = points.shape
    unit_cols = col_count // units
    eq_count = row_weight.shape[0]
    lanes = max(LANES, unit_cols // owners)
    left = capacity % 8
    tail = 0 < left <= 4
    groups = capacity // 8 + (left > 4)
    span = groups * desc + (desc // 2 if tail else 0) + LANES
    env_count = cores * owners * (8 * groups + 4 * tail)
    line = owners // 4
    vmem = pl.BlockSpec(memory_space=pltpu.VMEM)
    hbm = pl.BlockSpec(memory_space=pltpu.HBM)
    dma = pltpu.SemaphoreType.DMA
    return pl.pallas_call(
        functools.partial(fit_kernel, owners, cores, units, groups, tail),
        out_shape=(
            jax.ShapeDtypeStruct((units, PANELS, owners, PW, lanes), BF16),
            jax.ShapeDtypeStruct((units, eq_count, unit_cols), F32),
            jax.ShapeDtypeStruct((eq_count, WIDE), F32),
            jax.ShapeDtypeStruct((WIDE, WIDE), F32),
        ),
        in_specs=[hbm] * 7,
        out_specs=(vmem, vmem, vmem, vmem),
        scratch_shapes=[
            pltpu.VMEM(descriptors.shape, BF16),
            pltpu.VMEM((1, owner.shape[0]), jnp.int32),
            pltpu.VMEM((1, owner.shape[0]), jnp.int32),
            pltpu.VMEM((1, col_count), F32),
            pltpu.VMEM((1, eq_count), F32),
            pltpu.VMEM((1, LANES), F32),
            pltpu.VMEM((units, unit_cols, desc), BF16),
            pltpu.VMEM((WIDE, desc), BF16),
            pltpu.VMEM((1, WIDE), F32),
            pltpu.VMEM((2, owner.shape[0], LANES), F32),
            pltpu.VMEM((owners, 8, span), BF16),
            pltpu.VMEM((cores, owners, 8, span), BF16),
            pltpu.VMEM((env_count, desc), BF16),
            pltpu.VMEM((cores, eq_count // cores, WIDE), BF16),
            pltpu.VMEM((owners, cores, eq_count // cores, WIDE), BF16),
            pltpu.VMEM((units, owners, eq_count, lanes), BF16),
            pltpu.VMEM((units, owners, eq_count, lanes), BF16),
            pltpu.VMEM((units, PANELS, owners, PW, lanes), BF16),
            dma((6,)),
            dma((units,)),
            dma((units,)),
            dma,
            dma((2, cores)),
            dma((2,)),
            dma((owners,)),
            dma((owners,)),
            dma((cores, owners)),
            dma((cores, owners)),
            dma((owners,)),
            dma((owners,)),
            dma((cores, owners)),
            dma((cores, owners)),
            dma((units, owners)),
            dma((units, owners)),
            dma((units, PANELS, 3 + line)),
            dma((units, PANELS, 3 + line)),
        ],
        compiler_params=pltpu.CompilerParams(
            collective_id=0, has_side_effects=True, vmem_limit_bytes=FIT_VMEM
        ),
    )(
        *(
            pltpu.with_memory_space_constraint(value, pltpu.HBM)
            for value in (
                descriptors, owner.reshape(1, -1), struct.reshape(1, -1), points,
                scale.reshape(1, -1), row_weight.reshape(1, -1),
                jnp.broadcast_to(ridge.reshape(1, 1), (1, LANES)),
            )
        )
    )


def place_of(owner, unit, owners):
    first, second = unit % 2, (unit + 1) % 2
    return (
        (owner >> first) % 2 * (owners // 2) + (owner >> second) % 2 * (owners // 4) + owner // 4
    )


def finish_kernel(
    norm_scale, coupled, matrix, q_ref, r_head_ref, r_hbm, reduced_hbm,
    r_out, reduced_out, out_sem,
):
    units, _, owners, _, _ = coupled.shape
    unit_cols = matrix.shape[2]
    width = unit_cols // owners
    q_cols = q_ref[...]
    q_high, q_low = split_bf16(q_cols)
    q_wide = jnp.concatenate([q_high, q_low], axis=1)
    root = lax.axis_index("cols") == 0
    part = unit_cols // PARTS
    stores = []
    for u in range(units):
        for h in range(PARTS):
            mine = range(h * owners // PARTS, (h + 1) * owners // PARTS)
            block = jnp.concatenate(
                [
                    jnp.concatenate(
                        [coupled[u, k, place_of(p, u, owners)][:, :width] for p in mine], axis=1
                    )
                    for k in range(PANELS)
                ],
                axis=0,
            )
            update = mm(q_wide, jnp.concatenate([block, block], axis=0), ((1,), (0,)), None)
            at = slice(u * unit_cols + h * part, u * unit_cols + (h + 1) * part)
            r_out[:, at] = block.astype(F32) * norm_scale
            reduced_out[:, at] = matrix[u, :, h * part:(h + 1) * part] - update
            if u == 0 and h == 0:
                r_out[:, :WIDE] = jnp.where(root, r_head_ref[...] * norm_scale, r_out[:, :WIDE])
                reduced_out[:, :WIDE] = jnp.where(root, q_cols, reduced_out[:, :WIDE])
            for i, (src, dst) in enumerate(((r_out, r_hbm), (reduced_out, reduced_hbm))):
                store = pltpu.make_async_copy(
                    src.at[:, at], dst.at[:, at], out_sem.at[i, u * PARTS + h]
                )
                store.start()
                stores.append(store)
    for store in stores:
        store.wait()


def finish(coupled, matrix, q_cols, r_head, norm_scale):
    units = coupled.shape[0]
    _, eq_count, unit_cols = matrix.shape
    vmem = pl.BlockSpec(memory_space=pltpu.VMEM)
    hbm = pl.BlockSpec(memory_space=pltpu.HBM)
    r_shape = (WIDE, units * unit_cols)
    reduced_shape = (eq_count, units * unit_cols)
    return pl.pallas_call(
        functools.partial(finish_kernel, norm_scale),
        out_shape=(
            jax.ShapeDtypeStruct(r_shape, F32),
            jax.ShapeDtypeStruct(reduced_shape, F32),
        ),
        in_specs=[vmem] * 4,
        out_specs=(hbm, hbm),
        scratch_shapes=[
            pltpu.VMEM(r_shape, F32),
            pltpu.VMEM(reduced_shape, F32),
            pltpu.SemaphoreType.DMA((2, units * PARTS)),
        ],
        compiler_params=pltpu.CompilerParams(vmem_limit_bytes=FINISH_VMEM),
    )(coupled, matrix, q_cols, r_head)


def body(
    descriptors, sparse_points, point_scale, env_owner, env_structure, row_weight, ridge_factor
):
    owners, cores = lax.axis_size("rows"), lax.axis_size("cols")
    eq_count = row_weight.shape[0]
    env_local = descriptors.shape[0]
    col_count = sparse_points.shape[0]
    per_block = max(2, (3 * BLOCK + 2 * owners - 1) // (2 * owners))
    capacity = min(env_local, per_block * (-(-env_local // BLOCK)))
    units = max(1, min(UNITS, col_count // (LANES * owners)))
    coupled, matrix, q_cols, r_head = fit(
        descriptors, env_owner, env_structure, sparse_points, point_scale, row_weight,
        ridge_factor, owners, cores, units, capacity,
    )
    return finish(coupled, matrix, q_cols, r_head, 1.0 / math.sqrt(owners * eq_count))


def solution(mesh):
    return jax.shard_map(
        body,
        mesh=mesh,
        in_specs=(
            P(("rows", "cols"), None),
            P("cols", None),
            P("cols"),
            P("rows", None),
            P("rows"),
            P("rows"),
            P(),
        ),
        out_specs=(P(None, "cols"), P("rows", "cols")),
        check_vma=False,
    )
```

```python
import functools
import math

import jax
import jax.numpy as jnp
from jax import lax
from jax.experimental import pallas as pl
from jax.experimental.pallas import tpu as pltpu
from jax.sharding import PartitionSpec as P

PW = 64
PANELS = 2
WIDE = PW * PANELS
BLOCK = 128
LANES = 128
PIVOTS = 8
UNITS = 2
PARTS = 2
LAG = 0.9
FIT_VMEM = 44 << 20
FINISH_VMEM = 16 << 20
HI = lax.Precision.HIGHEST
F32 = jnp.float32
BF16 = jnp.bfloat16
MESH = pl.DeviceIdType.MESH


def mm(left, right, contract, precision=HI):
    return lax.dot_general(
        left, right, ((contract[0], contract[1]), ((), ())), precision=precision,
        preferred_element_type=F32,
    )


def eliminate(system):
    rows = lax.broadcasted_iota(jnp.int32, (PW, WIDE), 0)
    for k in range(0, PW, PIVOTS):
        rest, index = system[k:], rows[k:]
        cols = [
            jnp.broadcast_to(rest[:, k + j:k + j + 1], rest.shape) for j in range(PIVOTS)
        ]
        tops = [rest[j:j + 1] for j in range(PIVOTS)]
        for p in range(PIVOTS):
            mult = jnp.where(index > k + p, cols[p] * (1.0 / cols[p][p:p + 1]), 0.0)
            for j in range(p + 1, PIVOTS):
                cols[j] = cols[j] - mult * cols[j][p:p + 1]
                tops[j] = tops[j] - mult[j:j + 1] * tops[p]
            cols[p] = mult
        for p in range(PIVOTS):
            rest = rest - cols[p] * tops[p]
        system = jnp.concatenate([system[:k], rest], axis=0) if k else rest
    return system


def factor(gram, ridge):
    row = lax.broadcasted_iota(jnp.int32, (PW, PW), 0)
    col = lax.broadcasted_iota(jnp.int32, (PW, PW), 1)
    on = row == col
    trace = jnp.sum(jnp.sum(jnp.where(on, gram, 0.0), axis=1, keepdims=True), axis=0, keepdims=True)
    shift = ridge * trace / PW + 1e-06
    eye = on.astype(F32)
    system = eliminate(jnp.concatenate([gram + shift * eye, eye], axis=1))
    left = system[:, :PW]
    diag = jnp.sum(jnp.where(on, left, 0.0), axis=1, keepdims=True)
    scale = lax.rsqrt(diag)
    upper = jnp.where(col >= row, left * scale, 0.0)
    return upper, system[:, PW:] * scale, shift


def bit_of(index, bit):
    return (index // (1 << bit)) % 2


def split_bf16(value):
    high = value.astype(BF16)
    return high, (value - high.astype(F32)).astype(BF16)


def fit_kernel(
    owners, cores, units, groups, tail,
    desc_hbm, owner_hbm, struct_hbm, points_hbm, scale_hbm, weight_hbm, ridge_hbm,
    coupled_ref, matrix_ref, q_ref, r_head_ref,
    desc_ref, owner_ref, struct_ref, scale_ref, weight_ref, ridge_ref,
    points, head_points, head_scale, keys, parcel, landed, env,
    head_out, heads, block_out, block_in, whole,
    start_sem, points_sem, out_sem, root_sem, root_send, root_recv, e_send, e_recv, f_send, f_recv,
    h_send, h_recv, k_send, k_recv, b_send, b_recv, r_send, r_recv,
):
    me = lax.axis_index("rows")
    core = lax.axis_index("cols")
    env_local, desc = desc_ref.shape
    eq_count = weight_ref.shape[1]
    col_count = scale_ref.shape[1]
    unit_cols = col_count // units
    width = unit_cols // owners
    lanes = block_in.shape[3]
    share = eq_count // cores
    line = owners // 4
    half_desc = desc // 2

    barrier = pltpu.get_barrier_semaphore()

    def greet_rows(d, _):
        pl.semaphore_signal(
            barrier, inc=1, device_id={"rows": (me + d) % owners}, device_id_type=MESH
        )
        return 0

    def greet_cols(d, _):
        pl.semaphore_signal(
            barrier, inc=1, device_id={"cols": (core + d) % cores}, device_id_type=MESH
        )
        return 0

    lax.fori_loop(1, owners, greet_rows, 0)
    lax.fori_loop(1, cores, greet_cols, 0)

    inputs = (
        (owner_hbm, owner_ref), (struct_hbm, struct_ref), (desc_hbm, desc_ref),
        (scale_hbm, scale_ref), (weight_hbm, weight_ref), (ridge_hbm, ridge_ref),
    )
    inputs = [
        pltpu.make_async_copy(src, dst, start_sem.at[i]) for i, (src, dst) in enumerate(inputs)
    ]
    for load in inputs:
        load.start()
    loads = []
    for u in range(units):
        load = pltpu.make_async_copy(
            points_hbm.at[pl.ds(u * unit_cols, unit_cols)], points.at[u], points_sem.at[u]
        )
        load.start()
        loads.append(load)

    def as_column(row):
        return jnp.broadcast_to(row.astype(F32), (LANES, row.shape[1])).T

    for load in inputs:
        load.wait()
    keys[0] = as_column(owner_ref[...])
    keys[1] = as_column(struct_ref[...])
    mine = pl.ds(pl.multiple_of(core * env_local, 8), env_local)
    own, struct = keys[0, mine], keys[1, mine]
    lane = lax.broadcasted_iota(jnp.int32, (env_local, LANES), 1).astype(F32)
    named = own == lane
    before = (
        lax.broadcasted_iota(jnp.int32, (env_local, env_local), 0)
        > lax.broadcasted_iota(jnp.int32, (env_local, env_local), 1)
    )
    ahead = mm(
        jnp.where(before, 1.0, 0.0).astype(BF16), jnp.where(named, 1.0, 0.0).astype(BF16),
        ((1,), (0,)), None,
    )
    within = jnp.sum(jnp.where(named, ahead, 0.0), axis=1, keepdims=True)
    own, struct = own[:, :1], struct[:, :1]
    place = lax.broadcasted_iota(jnp.int32, (env_local, owners * 8), 1).astype(F32)

    def pick(first, count, shift):
        inside = (within >= first) & (within < first + count)
        spot_of = jnp.where(inside, own * 8 + (within - first) + shift, -1.0)
        return jnp.where(place == spot_of, 1.0, 0.0).astype(BF16)

    descriptors = desc_ref[...]
    label = jnp.zeros((owners * 8, LANES), F32)
    for g in range(groups):
        chosen = pick(8 * g, 8, 0)
        block = mm(chosen, descriptors, ((0,), (0,)), None)
        parcel[:, :, g * desc:(g + 1) * desc] = block.reshape(owners, 8, desc).astype(BF16)
        tag = jnp.where(lane == g, struct + 1.0, 0.0).astype(BF16)
        label = label + mm(chosen, tag, ((0,), (0,)), None)
    edge = groups * desc
    if tail:
        lower, upper = pick(8 * groups, 4, 0), pick(8 * groups, 4, 4)
        block = mm(lower, descriptors[:, :half_desc], ((0,), (0,)), None) + mm(
            upper, descriptors[:, half_desc:], ((0,), (0,)), None
        )
        parcel[:, :, edge:edge + half_desc] = block.reshape(owners, 8, half_desc).astype(BF16)
        tag = jnp.where(lane == groups, struct + 1.0, 0.0).astype(BF16)
        label = label + mm(lower, tag, ((0,), (0,)), None)
        edge = edge + half_desc
    parcel[:, :, edge:] = label.reshape(owners, 8, LANES).astype(BF16)

    pl.semaphore_wait(barrier, owners + cores - 2)

    def exchange(src_of, slot_of, send, recv):
        def copy(to, sender):
            return pltpu.make_async_remote_copy(
                src_ref=src_of(to), dst_ref=slot_of(sender), send_sem=send.at[to],
                recv_sem=recv.at[sender], device_id={"rows": to}, device_id_type=MESH,
            )

        def start(d, _):
            copy((me + d) % owners, me).start()
            return 0

        def end(d, _):
            other = (me + d) % owners
            copy(other, other).wait_send()
            copy(other, other).wait_recv()
            return 0

        return start, end, copy

    start, _, routed = exchange(
        lambda to: parcel.at[to], lambda sender: landed.at[core, sender], e_send, e_recv
    )
    lax.fori_loop(1, owners, start, 0)

    def root_copies(to):
        pair = []
        for i, (src, dst) in enumerate(
            ((points_hbm.at[pl.ds(0, WIDE)], head_points), (scale_ref.at[:, pl.ds(0, WIDE)], head_scale))
        ):
            pair.append(
                pltpu.make_async_remote_copy(
                    src_ref=src, dst_ref=dst, send_sem=root_send.at[i, to],
                    recv_sem=root_recv.at[i], device_id={"cols": to}, device_id_type=MESH,
                )
            )
        return pair

    own_points = pltpu.make_async_copy(points_hbm.at[pl.ds(0, WIDE)], head_points, root_sem)

    @pl.when(core == 0)
    def _():
        own_points.start()
        head_scale[...] = scale_ref[:, :WIDE]
        for to in range(1, cores):
            for copy in root_copies(to):
                copy.start()

    def pass_on(slot, to, sender):
        return pltpu.make_async_remote_copy(
            src_ref=landed.at[sender, slot], dst_ref=landed.at[sender, slot],
            send_sem=f_send.at[to, slot], recv_sem=f_recv.at[sender, slot],
            device_id={"cols": to}, device_id_type=MESH,
        )

    def pass_all(slot):
        def one(d, _):
            pass_on(slot, (core + d) % cores, core).start()
            return 0

        lax.fori_loop(1, cores, one, 0)

    landed[core, me] = parcel[me]
    pass_all(me)

    def land(d, _):
        other = (me + d) % owners
        routed(other, other).wait_recv()
        pass_all(other)
        return 0

    lax.fori_loop(1, owners, land, 0)

    @pl.when(core == 0)
    def _():
        own_points.wait()
        for to in range(1, cores):
            for copy in root_copies(to):
                copy.wait_send()

    @pl.when(core != 0)
    def _():
        for copy in root_copies(0):
            copy.wait_recv()

    def passed(i, _):
        slot = i % owners
        other = (core + 1 + i // owners) % cores
        pass_on(slot, other, other).wait_recv()
        return 0

    lax.fori_loop(0, owners * (cores - 1), passed, 0)

    targets = lax.broadcasted_iota(jnp.int32, (1, LANES), 1).astype(F32)
    low_half = lax.broadcasted_iota(jnp.int32, (owners // 2, 8, 1), 1) < 4
    marks = []
    row = 0

    def swap(value):
        return jnp.concatenate([value[:, 4:], value[:, :4]], axis=1)

    def evens(value):
        paired = value.reshape((owners // 2, 2) + value.shape[1:])
        return paired[:, 0], paired[:, 1]

    for c in range(cores):
        tags = landed[c, :, :, edge:].astype(F32)
        for g in range(groups):
            env[row:row + owners * 8] = landed[c, :, :, g * desc:(g + 1) * desc].astype(
                F32
            ).reshape(owners * 8, desc).astype(BF16)
            tag = tags[:, :, g:g + 1].reshape(owners * 8, 1) - 1.0
            marks.append(jnp.where(tag == targets, 1.0, 0.0))
            row += owners * 8
        if tail:
            first, second = evens(
                landed[c, :, :, groups * desc:groups * desc + half_desc].astype(F32)
            )
            left = jnp.where(low_half, first, swap(second))
            right = jnp.where(low_half, swap(first), second)
            env[row:row + owners * 4, :half_desc] = left.reshape(owners * 4, half_desc).astype(BF16)
            env[row:row + owners * 4, half_desc:] = right.reshape(owners * 4, half_desc).astype(BF16)
            first, second = evens(jnp.broadcast_to(tags[:, :, groups:groups + 1], tags.shape))
            tag = jnp.where(low_half, first, swap(second)).reshape(owners * 4, LANES) - 1.0
            marks.append(jnp.where(tag == targets, 1.0, 0.0))
            row += owners * 4
    selector = jnp.concatenate(marks, axis=0).T[:eq_count].astype(BF16)
    weight = as_column(weight_ref[...])[:, :1]

    def equations(rows, scale):
        products = mm(env[...], rows, ((1,), (1,)), None) * desc ** (-0.5)
        squared = products * products
        kernel = (scale * squared * squared).astype(BF16)
        return mm(selector, kernel, ((1,), (0,)), None) * weight

    head = equations(head_points[...], head_scale[...])
    for c in range(cores):
        head_out[c] = head[c * share:(c + 1) * share].astype(BF16)
    start, _, shared = exchange(
        lambda to: head_out.at[core], lambda sender: heads.at[sender, core], h_send, h_recv
    )
    lax.fori_loop(1, owners, start, 0)
    heads[me] = head_out[...]

    outs = []
    blocks = []
    for u in range(units):
        loads[u].wait()
        value = equations(points[u], scale_ref[:, u * unit_cols:(u + 1) * unit_cols])
        matrix_ref[u] = value
        value = value.astype(BF16)
        for p in range(owners):
            block_out[u, p, :, :width] = value[:, p * width:(p + 1) * width]
        start, end, _ = exchange(
            lambda to, u=u: block_out.at[u, to], lambda sender, u=u: block_in.at[u, sender],
            b_send.at[u], b_recv.at[u],
        )
        lax.fori_loop(1, owners, start, 0)
        block_in[u, me] = block_out[u, me]
        blocks.append(end)

    def hand_head(slot, to, sender):
        part = heads.at[slot, sender]
        return pltpu.make_async_remote_copy(
            src_ref=part, dst_ref=part, send_sem=k_send.at[to, slot],
            recv_sem=k_recv.at[sender, slot], device_id={"cols": to}, device_id_type=MESH,
        )

    def land_head(d, _):
        other = (me + d) % owners
        shared(other, other).wait_recv()

        def one(e, _):
            hand_head(other, (core + e) % cores, core).start()
            return 0

        lax.fori_loop(1, cores, one, 0)
        return 0

    lax.fori_loop(1, owners, land_head, 0)

    def handed(i, _):
        other = (core + 1 + i // (owners - 1)) % cores
        hand_head((me + 1 + i % (owners - 1)) % owners, other, other).wait_recv()
        return 0

    lax.fori_loop(0, (owners - 1) * (cores - 1), handed, 0)

    every = heads[...].astype(F32).reshape(owners * eq_count, WIDE).T.astype(BF16)
    gram = mm(every, every, ((1,), (1,)), None)
    ridge = ridge_ref[:, :1]
    up1, inv1, shift = factor(gram[:PW, :PW], ridge)
    c12 = mm(inv1, gram[:PW, PW:], ((1,), (0,)))
    back = mm(inv1, c12, ((0,), (0,)))
    pair = jnp.concatenate([c12, jnp.sqrt(shift) * back], axis=0)
    deep = c12 + shift * mm(inv1, back, ((1,), (0,)))
    up2, inv2, _ = factor(gram[PW:, PW:] - mm(pair, pair, ((0,), (0,))), ridge)
    q1 = mm(head[:, :PW], inv1, ((1,), (1,)))
    q2 = mm(head[:, PW:] - mm(q1, c12, ((1,), (0,))), inv2, ((1,), (1,)))
    q_ref[...] = jnp.concatenate([q1, q2], axis=1)
    r_head_ref[...] = jnp.concatenate(
        [
            jnp.concatenate([up1, c12], axis=1),
            jnp.concatenate([jnp.zeros((PW, PW), F32), up2], axis=1),
        ],
        axis=0,
    )

    rank = me // 4

    def bit(u, t):
        return (t + u) % 2

    def start_of(u, t):
        return sum(
            (bit_of(me, bit(u, i)) * (owners >> (i + 1)) for i in range(t)), jnp.int32(0)
        )

    def peer(u, t):
        return me + (1 - 2 * bit_of(me, bit(u, t))) * (1 << bit(u, t))

    def piece_copy(u, k, t, slot):
        part = whole.at[u, k, start_of(u, 2) + slot]
        index = 1 + (1 + t) * line + slot
        return pltpu.make_async_remote_copy(
            src_ref=part, dst_ref=part, send_sem=r_send.at[u, k, index],
            recv_sem=r_recv.at[u, k, index], device_id={"rows": peer(u, t)}, device_id_type=MESH,
        )

    def quarter_copy(u, k):
        quarter = owners // 4
        at = start_of(u, 1) + (1 - bit_of(me, bit(u, 1))) * quarter
        part = whole.at[u, k, pl.ds(at, quarter)]
        return pltpu.make_async_remote_copy(
            src_ref=part, dst_ref=part, send_sem=r_send.at[u, k, 0],
            recv_sem=r_recv.at[u, k, 0], device_id={"rows": peer(u, 0)}, device_id_type=MESH,
        )

    def line_copy(u, k, to, sender):
        part = whole.at[u, k, start_of(u, 2) + sender]
        return pltpu.make_async_remote_copy(
            src_ref=part, dst_ref=part, send_sem=r_send.at[u, k, 1 + to],
            recv_sem=r_recv.at[u, k, 1 + sender],
            device_id={"rows": to * 4 + me % 4}, device_id_type=MESH,
        )

    others = [(rank + d) % line for d in range(1, line)]

    def open_piece(u, k, value):
        whole[u, k, start_of(u, 2) + rank] = value.astype(BF16)
        for to in others:
            line_copy(u, k, to, rank).start()
        for t in (1, 0):
            piece_copy(u, k, t, rank).start()

    def open_unit(u):
        lax.fori_loop(1, owners, blocks[u], 0)
        block = block_in[u].astype(F32).reshape(owners * eq_count, lanes).astype(BF16)
        cross = mm(every, block, ((1,), (0,)), None)
        first = mm(inv1, cross[:PW], ((1,), (0,)))
        open_piece(u, 0, first)
        rest = cross[PW:] - mm(deep, first, ((0,), (0,)))
        open_piece(u, 1, mm(inv2, rest, ((1,), (0,))))

    def line_end(u):
        for k in range(PANELS):
            for other in others:
                line_copy(u, k, other, other).wait_recv()
                for t in (1, 0):
                    piece_copy(u, k, t, other).start()

    def middle(u):
        for k in range(PANELS):
            for slot in range(line):
                piece_copy(u, k, 1, slot).wait_recv()
            quarter_copy(u, k).start()

    def last(u):
        for k in range(PANELS):
            for slot in range(line):
                piece_copy(u, k, 0, slot).wait_recv()
            quarter_copy(u, k).wait_recv()
        out = pltpu.make_async_copy(whole.at[u], coupled_ref.at[u], out_sem.at[u])
        out.start()
        outs.append(out)

    steps = (open_unit, line_end, middle, last)
    plan = sorted((s + LAG * u, u, s) for u in range(units) for s in range(len(steps)))
    for _, u, s in plan:
        steps[s](u)

    for u in range(units):
        for k in range(PANELS):
            for slot in range(line):
                for t in (1, 0):
                    piece_copy(u, k, t, slot).wait_send()
            quarter_copy(u, k).wait_send()
            for to in others:
                line_copy(u, k, to, rank).wait_send()
    for out in outs:
        out.wait()

    def drain(d, _):
        other = (me + d) % owners
        routed(other, other).wait_send()
        shared(other, other).wait_send()
        return 0

    lax.fori_loop(1, owners, drain, 0)

    def drain_pass(i, _):
        pass_on(i % owners, (core + 1 + i // owners) % cores, core).wait_send()
        return 0

    lax.fori_loop(0, owners * (cores - 1), drain_pass, 0)

    def drain_head(i, _):
        to = (core + 1 + i // (owners - 1)) % cores
        hand_head((me + 1 + i % (owners - 1)) % owners, to, core).wait_send()
        return 0

    lax.fori_loop(0, (owners - 1) * (cores - 1), drain_head, 0)


def fit(descriptors, owner, struct, points, scale, row_weight, ridge, owners, cores, units, capacity):
    col_count, desc = points.shape
    unit_cols = col_count // units
    eq_count = row_weight.shape[0]
    lanes = max(LANES, unit_cols // owners)
    left = capacity % 8
    tail = 0 < left <= 4
    groups = capacity // 8 + (left > 4)
    span = groups * desc + (desc // 2 if tail else 0) + LANES
    env_count = cores * owners * (8 * groups + 4 * tail)
    line = owners // 4
    vmem = pl.BlockSpec(memory_space=pltpu.VMEM)
    hbm = pl.BlockSpec(memory_space=pltpu.HBM)
    dma = pltpu.SemaphoreType.DMA
    return pl.pallas_call(
        functools.partial(fit_kernel, owners, cores, units, groups, tail),
        out_shape=(
            jax.ShapeDtypeStruct((units, PANELS, owners, PW, lanes), BF16),
            jax.ShapeDtypeStruct((units, eq_count, unit_cols), F32),
            jax.ShapeDtypeStruct((eq_count, WIDE), F32),
            jax.ShapeDtypeStruct((WIDE, WIDE), F32),
        ),
        in_specs=[hbm] * 7,
        out_specs=(vmem, vmem, vmem, vmem),
        scratch_shapes=[
            pltpu.VMEM(descriptors.shape, BF16),
            pltpu.VMEM((1, owner.shape[0]), jnp.int32),
            pltpu.VMEM((1, owner.shape[0]), jnp.int32),
            pltpu.VMEM((1, col_count), F32),
            pltpu.VMEM((1, eq_count), F32),
            pltpu.VMEM((1, LANES), F32),
            pltpu.VMEM((units, unit_cols, desc), BF16),
            pltpu.VMEM((WIDE, desc), BF16),
            pltpu.VMEM((1, WIDE), F32),
            pltpu.VMEM((2, owner.shape[0], LANES), F32),
            pltpu.VMEM((owners, 8, span), BF16),
            pltpu.VMEM((cores, owners, 8, span), BF16),
            pltpu.VMEM((env_count, desc), BF16),
            pltpu.VMEM((cores, eq_count // cores, WIDE), BF16),
            pltpu.VMEM((owners, cores, eq_count // cores, WIDE), BF16),
            pltpu.VMEM((units, owners, eq_count, lanes), BF16),
            pltpu.VMEM((units, owners, eq_count, lanes), BF16),
            pltpu.VMEM((units, PANELS, owners, PW, lanes), BF16),
            dma((6,)),
            dma((units,)),
            dma((units,)),
            dma,
            dma((2, cores)),
            dma((2,)),
            dma((owners,)),
            dma((owners,)),
            dma((cores, owners)),
            dma((cores, owners)),
            dma((owners,)),
            dma((owners,)),
            dma((cores, owners)),
            dma((cores, owners)),
            dma((units, owners)),
            dma((units, owners)),
            dma((units, PANELS, 1 + 3 * line)),
            dma((units, PANELS, 1 + 3 * line)),
        ],
        compiler_params=pltpu.CompilerParams(
            collective_id=0, has_side_effects=True, vmem_limit_bytes=FIT_VMEM
        ),
    )(
        *(
            pltpu.with_memory_space_constraint(value, pltpu.HBM)
            for value in (
                descriptors, owner.reshape(1, -1), struct.reshape(1, -1), points,
                scale.reshape(1, -1), row_weight.reshape(1, -1),
                jnp.broadcast_to(ridge.reshape(1, 1), (1, LANES)),
            )
        )
    )


def place_of(owner, unit, owners):
    first, second = unit % 2, (unit + 1) % 2
    return (
        (owner >> first) % 2 * (owners // 2) + (owner >> second) % 2 * (owners // 4) + owner // 4
    )


def finish_kernel(
    norm_scale, coupled, matrix, q_ref, r_head_ref, r_hbm, reduced_hbm,
    r_out, reduced_out, out_sem,
):
    units, _, owners, _, _ = coupled.shape
    unit_cols = matrix.shape[2]
    width = unit_cols // owners
    q_cols = q_ref[...]
    q_high, q_low = split_bf16(q_cols)
    q_wide = jnp.concatenate([q_high, q_low], axis=1)
    root = lax.axis_index("cols") == 0
    part = unit_cols // PARTS
    stores = []
    for u in range(units):
        for h in range(PARTS):
            mine = range(h * owners // PARTS, (h + 1) * owners // PARTS)
            block = jnp.concatenate(
                [
                    jnp.concatenate(
                        [coupled[u, k, place_of(p, u, owners)][:, :width] for p in mine], axis=1
                    )
                    for k in range(PANELS)
                ],
                axis=0,
            )
            update = mm(q_wide, jnp.concatenate([block, block], axis=0), ((1,), (0,)), None)
            at = slice(u * unit_cols + h * part, u * unit_cols + (h + 1) * part)
            r_out[:, at] = block.astype(F32) * norm_scale
            reduced_out[:, at] = matrix[u, :, h * part:(h + 1) * part] - update
            if u == 0 and h == 0:
                r_out[:, :WIDE] = jnp.where(root, r_head_ref[...] * norm_scale, r_out[:, :WIDE])
                reduced_out[:, :WIDE] = jnp.where(root, q_cols, reduced_out[:, :WIDE])
            for i, (src, dst) in enumerate(((r_out, r_hbm), (reduced_out, reduced_hbm))):
                store = pltpu.make_async_copy(
                    src.at[:, at], dst.at[:, at], out_sem.at[i, u * PARTS + h]
                )
                store.start()
                stores.append(store)
    for store in stores:
        store.wait()


def finish(coupled, matrix, q_cols, r_head, norm_scale):
    units = coupled.shape[0]
    _, eq_count, unit_cols = matrix.shape
    vmem = pl.BlockSpec(memory_space=pltpu.VMEM)
    hbm = pl.BlockSpec(memory_space=pltpu.HBM)
    r_shape = (WIDE, units * unit_cols)
    reduced_shape = (eq_count, units * unit_cols)
    return pl.pallas_call(
        functools.partial(finish_kernel, norm_scale),
        out_shape=(
            jax.ShapeDtypeStruct(r_shape, F32),
            jax.ShapeDtypeStruct(reduced_shape, F32),
        ),
        in_specs=[vmem] * 4,
        out_specs=(hbm, hbm),
        scratch_shapes=[
            pltpu.VMEM(r_shape, F32),
            pltpu.VMEM(reduced_shape, F32),
            pltpu.SemaphoreType.DMA((2, units * PARTS)),
        ],
        compiler_params=pltpu.CompilerParams(vmem_limit_bytes=FINISH_VMEM),
    )(coupled, matrix, q_cols, r_head)


def body(
    descriptors, sparse_points, point_scale, env_owner, env_structure, row_weight, ridge_factor
):
    owners, cores = lax.axis_size("rows"), lax.axis_size("cols")
    eq_count = row_weight.shape[0]
    env_local = descriptors.shape[0]
    col_count = sparse_points.shape[0]
    per_block = max(2, (3 * BLOCK + 2 * owners - 1) // (2 * owners))
    capacity = min(env_local, per_block * (-(-env_local // BLOCK)))
    units = max(1, min(UNITS, col_count // (LANES * owners)))
    coupled, matrix, q_cols, r_head = fit(
        descriptors, env_owner, env_structure, sparse_points, point_scale, row_weight,
        ridge_factor, owners, cores, units, capacity,
    )
    return finish(coupled, matrix, q_cols, r_head, 1.0 / math.sqrt(owners * eq_count))


def solution(mesh):
    return jax.shard_map(
        body,
        mesh=mesh,
        in_specs=(
            P(("rows", "cols"), None),
            P("cols", None),
            P("cols"),
            P("rows", None),
            P("rows"),
            P("rows"),
            P(),
        ),
        out_specs=(P(None, "cols"), P("rows", "cols")),
        check_vma=False,
    )
```
